128 devices in a mesh: comp: 128 (over z, y, x, core).
Axes of the slice: x: 4, y: 4, z: 4, core: 2. Of those that a mesh axis runs over, the one named last changes fastest.
Arguments:
- src_fields: float32 [32768, 320], P('comp'), may hold values from -6 to 6
- weights: float32 [512, 256, 512], P('comp'), may hold values from -0.25 to 0.25
- block_src: int32 [512, 512], P('comp'), may hold values from 0 to 1023, as said below
- send_src: int32 [16384, 8], P('comp'), may hold values from 0 to 255, as said below
- coupler_send: int32 [16384, 16], P('comp'), may hold values from 0 to 1023, as said below
- ocean_from: int32 [131072], P('comp'), may hold values from 0 to 2047, as said below
- surface_temp: float32 [131072], P('comp'), may hold values from -4 to 4
- ocean_current: float32 [2, 131072], P(None, 'comp'), may hold values from -3 to 3
Outputs:
- remapped: float32 [131072, 320], P('comp')
- fluxes: float32 [4, 131072], P(None, 'comp')
The draws below stay inside these ranges and needn't reach their ends.
Inputs may be any that keep to these rules, and one draw needn't show every extreme that they name: `block_src`: slots at positions below the pair's row count hold data; counts from one source device to one coupler reach 8 for some pair in every row and column of the count table, every coupler receives 2 * 256 rows, every block column names a filled slot, and every coupler's and every source device's counts form the same multiset. `send_src`: entries within one row are distinct. `coupler_send`: each coupler sends each of its 1024 rows exactly once; counts from one coupler to one ocean device reach 16 in every row and column of the count table and form the same multiset for every coupler and every ocean device; unfilled slots hold 0. `ocean_from`: each ocean device's entries are its 1024 filled receive slots, each once.
All inputs are finite; a program needn't handle non-finite values.
Results may differ from the reference program's by a relative error of at most 0.0003.
Values sent between devices are 32-bit elements; how exact they have to be, the bound alone decides.
No kernel may reach another device: no remote copies, remote signals or barrier semaphores. Data moves between devices by JAX's collectives and lax.ppermute only.
A program may use at most 64 MiB of HBM per device.

```python
import jax
import jax.numpy as jnp
from jax import lax

FIELDS = 40
LEV = 8
OB = 256
SB = 512
SRC_DEV = 256
OCN_DEV = 1024
NBLK = 4
CAP = 8
CAP2 = 16
SRC = 32768
OCN = 131072
N_COMP = 128


def counts_table(key, middle):
    half = N_COMP // 2
    key_delta, key_rows, key_cols = jax.random.split(key, 3)
    delta = jax.random.randint(key_delta, (half,), 0, middle + 1).astype(jnp.int32)
    delta = delta.at[0].set(middle)
    values = jnp.concatenate([middle + delta, middle - delta]).astype(jnp.int32)
    row_perm = jax.random.permutation(key_rows, N_COMP).astype(jnp.int32)
    col_perm = jax.random.permutation(key_cols, N_COMP).astype(jnp.int32)
    latin = (row_perm[:, None] + col_perm[None, :]) % N_COMP
    return values[latin]


def source_counts(key):
    return counts_table(jax.random.fold_in(key, 11), CAP // 2)


def ocean_counts(key):
    return counts_table(jax.random.fold_in(key, 21), CAP2 // 2)


def draw_send_src(key, part):
    keys = jax.random.split(jax.random.fold_in(key, 12), N_COMP * N_COMP)

    def one_row(row_key):
        return jax.random.permutation(row_key, SRC_DEV)[:CAP].astype(jnp.int32)
    return jax.vmap(one_row)(keys)


def draw_block_src(key, part):
    counts = source_counts(key)
    keys = jax.random.split(jax.random.fold_in(key, 13), N_COMP)
    total = 2 * SRC_DEV

    def one_coupler(dest):
        column = counts[:, dest]
        cumul = jnp.cumsum(column).astype(jnp.int32)
        picks = jax.random.randint(keys[dest], (NBLK * SB,), 0, total).astype(jnp.int32)
        picks = picks.at[0].set(total - 1).at[1].set(0)
        sender = jnp.searchsorted(cumul, picks, side='right').astype(jnp.int32)
        start = cumul[sender] - column[sender]
        return (sender * CAP + picks - start).reshape(NBLK, SB).astype(jnp.int32)
    return lax.map(one_coupler, jnp.arange(N_COMP, dtype=jnp.int32)).reshape(N_COMP * NBLK, SB)


def draw_coupler_send(key, part):
    counts = ocean_counts(key)
    keys = jax.random.split(jax.random.fold_in(key, 22), N_COMP)

    def one_coupler(dest):
        row = counts[dest]
        offset = jnp.cumsum(row) - row
        slot = jnp.arange(CAP2, dtype=jnp.int32)
        place = offset[:, None] + slot[None, :]
        filled = slot[None, :] < row[:, None]
        order = jax.random.permutation(keys[dest], OCN_DEV).astype(jnp.int32)
        return jnp.where(filled, order[jnp.minimum(place, OCN_DEV - 1)], 0).astype(jnp.int32)
    return lax.map(one_coupler, jnp.arange(N_COMP, dtype=jnp.int32)).reshape(N_COMP * N_COMP, CAP2)


def draw_ocean_from(key, part):
    counts = ocean_counts(key)
    keys = jax.random.split(jax.random.fold_in(key, 23), N_COMP)

    def one_ocean(owner):
        column = counts[:, owner]
        cumul = jnp.cumsum(column).astype(jnp.int32)
        places = jnp.arange(OCN_DEV, dtype=jnp.int32)
        coupler = jnp.searchsorted(cumul, places, side='right').astype(jnp.int32)
        start = cumul[coupler] - column[coupler]
        flat_slot = (coupler * CAP2 + places - start).astype(jnp.int32)
        order = jax.random.permutation(keys[owner], OCN_DEV).astype(jnp.int32)
        return flat_slot[order]
    return lax.map(one_ocean, jnp.arange(N_COMP, dtype=jnp.int32)).reshape(N_COMP * OCN_DEV)


def steps_of(stream_key, dims, cuts, low, largest):
    loudness = 1.0
    for dim, blocks in cuts:
        steps = jax.random.uniform(jax.random.fold_in(jax.random.fold_in(stream_key, 6), dim), (blocks,), jnp.float32, low / len(cuts), largest / len(cuts))
        loudness = loudness * jnp.repeat(jnp.exp(steps), dims[dim] // blocks).reshape((-1,) + (1,) * (len(dims) - 1 - dim))
    return loudness


def centred(key, shape, spread, reach, shards=(), held_as=jnp.bfloat16):
    drawn = jax.random.normal(key, shape, jnp.float32) * spread
    if len(shards) > 0:
        drawn = steps_of(key, shape, shards, -0.22, 0.18) * drawn
    return jnp.clip(drawn, min=-reach, max=reach).astype(held_as)


def setup_inputs(seed: int = 0) -> dict:
    key_list = jax.random.split(jax.random.key(seed), 9)
    return {
        "src_fields": centred(key_list[0], (SRC, FIELDS * LEV), 1.0, 6.0, ((0, 128),), jnp.float32),
        "weights": centred(key_list[1], (N_COMP * NBLK, OB, SB), SB ** -0.5, 0.25, ((0, 128),), jnp.float32),
        "block_src": draw_block_src(jax.random.fold_in(key_list[8], 71), 0),
        "send_src": draw_send_src(jax.random.fold_in(key_list[8], 71), 0),
        "coupler_send": draw_coupler_send(jax.random.fold_in(key_list[8], 71), 0),
        "ocean_from": draw_ocean_from(jax.random.fold_in(key_list[8], 71), 0),
        "surface_temp": centred(key_list[6], (OCN,), 1.0, 4.0, ((0, 128),), jnp.float32),
        "ocean_current": centred(key_list[7], (2, OCN), 0.5, 3.0, ((1, 128),), jnp.float32),
    }


def reference(src_fields, weights, block_src, send_src, coupler_send, ocean_from, surface_temp, ocean_current):
    columns = src_fields.shape[1]

    def coupler_block(dest):
        slots = lax.dynamic_slice_in_dim(block_src, dest * NBLK, NBLK, 0)
        sender = slots // CAP
        within = slots % CAP
        local_row = send_src[sender * N_COMP + dest, within]
        global_row = (sender * SRC_DEV + local_row).astype(jnp.int32)
        picked = jnp.take(src_fields, global_row.reshape(-1), axis=0).reshape(NBLK, SB, columns)
        block_w = lax.dynamic_slice_in_dim(weights, dest * NBLK, NBLK, 0)
        coupled = jnp.einsum('bos,bsw->bow', block_w, picked, precision=lax.Precision.HIGHEST, preferred_element_type=jnp.float32)
        return coupled.reshape(NBLK * OB, columns)
    all_rows = lax.map(coupler_block, jnp.arange(N_COMP, dtype=jnp.int32))
    owner = jnp.arange(N_COMP * OCN_DEV, dtype=jnp.int32) // OCN_DEV
    coupler = ocean_from // CAP2
    position = ocean_from % CAP2
    result_row = coupler_send[coupler * N_COMP + owner, position]
    remapped = jnp.take(all_rows.reshape(-1, columns), (coupler * OCN_DEV + result_row).astype(jnp.int32), axis=0)
    wind_east = remapped[:, 0]
    wind_north = remapped[:, LEV]
    air_temp = remapped[:, 2 * LEV]
    humidity = remapped[:, 3 * LEV]
    speed = jnp.sqrt(wind_east * wind_east + wind_north * wind_north + 1.0)
    saturated = 0.5 * jnp.exp(0.2 * surface_temp)
    fluxes = jnp.stack([0.6 * speed * (air_temp - surface_temp), 0.6 * speed * (humidity - saturated), 0.6 * speed * (wind_east - ocean_current[0]), 0.6 * speed * (wind_north - ocean_current[1])])
    return (remapped, fluxes)
```

```python
import jax
import jax.numpy as jnp
from jax import lax
from jax.experimental import pallas as pl
from jax.experimental.pallas import tpu as pltpu
from jax.sharding import PartitionSpec as P

LEV = 8
LANES = 128
HALF = LANES // 2
BF16 = jnp.bfloat16
F32 = jnp.float32


def split(x):
    high = x.astype(BF16)
    low = (x - high.astype(F32)).astype(BF16)
    return high, low


def dot(a, b, dims):
    return lax.dot_general(a, b, (dims, ((), ())), preferred_element_type=F32)


def gather_kernel(send_ref, src_ref, out_ref):
    slots, devices = send_ref.shape
    rows = src_ref.shape[1]
    high, low = split(src_ref[...])
    picks = send_ref[...].T
    stride = slots * 5 // 2
    tails = []
    for k in range(slots):
        hot = jnp.where(
            lax.broadcasted_iota(jnp.int32, (devices, rows), 1) == picks[:, k : k + 1], 1.0, 0.0
        ).astype(BF16)
        taken = dot(hot, high, ((1,), (1,))) + dot(hot, low, ((1,), (1,)))
        out_ref[pl.ds(k, devices, stride=stride), :] = taken[:, :LANES]
        out_ref[pl.ds(slots + k, devices, stride=stride), :] = taken[:, LANES : 2 * LANES]
        tails.append(taken[:, 2 * LANES :])
    for k in range(slots // 2):
        both = jnp.concatenate([tails[k], tails[k + slots // 2]], axis=1)
        out_ref[pl.ds(2 * slots + k, devices, stride=stride), :] = both


def spread_kernel(slots, src_ref, weights_ref, high_ref, low_ref):
    blocks, block_rows, block_cols = weights_ref.shape
    total = high_ref.shape[1]
    senders = total // slots
    for b in range(blocks):
        slot = src_ref[b : b + 1, :]
        column = (slot % slots) * senders + slot // slots
        hot = jnp.where(
            lax.broadcasted_iota(jnp.int32, (total, block_cols), 0) == column, 1.0, 0.0
        ).astype(BF16)
        high, low = split(weights_ref[b])
        summed = dot(high, hot, ((1,), (1,))) + dot(low, hot, ((1,), (1,)))
        high, low = split(summed)
        high_ref[pl.ds(b * block_rows, block_rows), :] = high
        low_ref[pl.ds(b * block_rows, block_rows), :] = low


def couple_kernel(slots, send_ref, high_ref, low_ref, recv_ref, out_ref, first_ref, second_ref, tail_ref):
    senders = high_ref.shape[1] // slots
    stride = slots * 5 // 2
    heads, tails = [], []
    for k in range(slots):
        heads.append(
            jnp.concatenate(
                [
                    recv_ref[pl.ds(k, senders, stride=stride), :],
                    recv_ref[pl.ds(slots + k, senders, stride=stride), :],
                ],
                axis=1,
            )
        )
    for k in range(slots // 2):
        both = recv_ref[pl.ds(2 * slots + k, senders, stride=stride), :]
        tails.append(both)
    lane = lax.broadcasted_iota(jnp.int32, (senders, LANES), 1)
    lower = [jnp.where(lane < HALF, t, pltpu.roll(t, HALF, 1)) for t in tails]
    upper = [jnp.where(lane < HALF, pltpu.roll(t, HALF, 1), t) for t in tails]
    head_high, head_low = split(jnp.concatenate(heads, axis=0))
    tail_high, tail_low = split(jnp.concatenate(lower + upper, axis=0))
    high, low = high_ref[...], low_ref[...]
    contract = ((1,), (0,))
    head = dot(high, head_high, contract) + dot(high, head_low, contract) + dot(low, head_high, contract)
    first_ref[...] = head[:, :LANES]
    second_ref[...] = head[:, LANES:]
    tail_ref[...] = dot(high, tail_high, contract) + dot(high, tail_low, contract) + dot(low, tail_high, contract)

    oceans = send_ref.shape[1]
    slots2 = send_ref.shape[0]
    wide = slots2 * 5 // 2
    left = lax.broadcasted_iota(jnp.int32, (1, LANES), 1) < HALF

    def one_ocean(o, carry):
        base = pl.multiple_of(o * wide, 8)
        rows = [send_ref[k, o] for k in range(slots2)]
        for k in range(slots2):
            out_ref[pl.ds(base + k, 1), :] = first_ref[pl.ds(rows[k], 1), :]
            out_ref[pl.ds(base + slots2 + k, 1), :] = second_ref[pl.ds(rows[k], 1), :]
        for k in range(slots2 // 2):
            out_ref[pl.ds(base + 2 * slots2 + k, 1), :] = jnp.where(
                left, tail_ref[pl.ds(rows[k], 1), :], tail_ref[pl.ds(rows[k + slots2 // 2], 1), :]
            )
        return carry

    lax.fori_loop(0, oceans, one_ocean, 0)


def place_kernel(slots2, from_ref, lane_ref, temp_ref, current_ref, arrived_ref, out_ref, flux_ref, first_ref, second_ref, tail_ref):
    cells = out_ref.shape[1]
    wide = slots2 * 5 // 2
    half = slots2 // 2
    unroll = 16

    def some(step, carry):
        base = pl.multiple_of(step * unroll, unroll)
        for j in range(unroll):
            slot = from_ref[base + j]
            row = (slot // slots2) * wide
            k = slot % slots2
            first_ref[pl.ds(base + j, 1), :] = arrived_ref[pl.ds(row + k, 1), :]
            second_ref[pl.ds(base + j, 1), :] = arrived_ref[pl.ds(row + slots2 + k, 1), :]
            tail_ref[pl.ds(base + j, 1), :] = arrived_ref[pl.ds(row + 2 * slots2 + k % half, 1), :]
        return carry

    lax.fori_loop(0, cells // unroll, some, 0)
    first = first_ref[...].T
    out_ref[:LANES, :] = first
    out_ref[LANES : 2 * LANES, :] = second_ref[...].T
    tail = tail_ref[...].T
    lower = lane_ref[...] % slots2 < half
    out_ref[2 * LANES :, :] = jnp.where(lower, tail[:HALF], tail[HALF:])
    wind_east = first[0:1]
    wind_north = first[LEV : LEV + 1]
    air_temp = first[2 * LEV : 2 * LEV + 1]
    humidity = first[3 * LEV : 3 * LEV + 1]
    surface = temp_ref[...]
    scale = 0.6 * jnp.sqrt(wind_east * wind_east + wind_north * wind_north + 1.0)
    flux_ref[0:1, :] = scale * (air_temp - surface)
    flux_ref[1:2, :] = scale * (humidity - 0.5 * jnp.exp(0.2 * surface))
    flux_ref[2:3, :] = scale * (wind_east - current_ref[0:1, :])
    flux_ref[3:4, :] = scale * (wind_north - current_ref[1:2, :])


def vmem():
    return pl.BlockSpec(memory_space=pltpu.VMEM)


def smem():
    return pl.BlockSpec(memory_space=pltpu.SMEM)


def params():
    return pltpu.CompilerParams(vmem_limit_bytes=48 * 1024 * 1024)


def exchange(flat, devices):
    rows = flat.shape[0] // devices
    shaped = flat.reshape(devices, rows // 4, 4, LANES)
    moved = lax.all_to_all(shaped, "comp", split_axis=0, concat_axis=0, tiled=True)
    return moved.reshape(flat.shape)


def shards(
    src_fields, weights, block_src, send_src, coupler_send, ocean_from, surface_temp, ocean_current
):
    devices = lax.axis_size("comp")
    slots, slots2 = send_src.shape[1], coupler_send.shape[1]
    blocks, block_rows, block_cols = weights.shape
    columns = src_fields.shape[1]
    cells = ocean_from.shape[0]
    total = devices * slots
    coupled = blocks * block_rows

    outgoing = pl.pallas_call(
        gather_kernel,
        out_shape=jax.ShapeDtypeStruct((devices * slots * 5 // 2, LANES), F32),
        in_specs=[vmem(), vmem()],
        out_specs=vmem(),
        compiler_params=params(),
        name="gather_rows",
    )(send_src.T, src_fields.T)
    received = exchange(outgoing, devices)

    high, low = pl.pallas_call(
        lambda *refs: spread_kernel(slots, *refs),
        out_shape=[jax.ShapeDtypeStruct((coupled, total), BF16)] * 2,
        in_specs=[vmem(), vmem()],
        out_specs=[vmem(), vmem()],
        compiler_params=params(),
        name="spread_weights",
    )(block_src, weights)

    leaving = pl.pallas_call(
        lambda *refs: couple_kernel(slots, *refs),
        out_shape=jax.ShapeDtypeStruct((devices * slots2 * 5 // 2, LANES), F32),
        in_specs=[smem(), vmem(), vmem(), vmem()],
        out_specs=vmem(),
        scratch_shapes=[pltpu.VMEM((coupled, LANES), F32)] * 3,
        compiler_params=params(),
        name="couple",
    )(coupler_send.T, high, low, received)
    arrived = exchange(leaving, devices)

    remapped, fluxes = pl.pallas_call(
        lambda *refs: place_kernel(slots2, *refs),
        out_shape=[jax.ShapeDtypeStruct((columns, cells), F32), jax.ShapeDtypeStruct((4, cells), F32)],
        in_specs=[smem(), vmem(), vmem(), vmem(), vmem()],
        out_specs=[vmem(), vmem()],
        scratch_shapes=[pltpu.VMEM((cells, LANES), F32)] * 3,
        compiler_params=params(),
        name="place",
    )(ocean_from, ocean_from[None], surface_temp[None], ocean_current, arrived)
    return (remapped.T, fluxes)


def solution(mesh):
    return jax.shard_map(
        shards,
        mesh=mesh,
        in_specs=(
            P("comp", None),
            P("comp", None, None),
            P("comp", None),
            P("comp", None),
            P("comp", None),
            P("comp"),
            P("comp"),
            P(None, "comp"),
        ),
        out_specs=(P("comp", None), P(None, "comp")),
        check_vma=False,
    )
```

```python
import jax
import jax.numpy as jnp
from jax import lax
from jax.experimental import pallas as pl
from jax.experimental.pallas import tpu as pltpu
from jax.sharding import PartitionSpec as P

LEV = 8
LANES = 128
HALF = LANES // 2
SUB = 8
BF16 = jnp.bfloat16
F32 = jnp.float32
I32 = jnp.int32
MIB = 1024 * 1024


def split(x):
    high = x.astype(BF16)
    low = (x - high.astype(F32)).astype(BF16)
    return high, low


def dot(a, b, dims):
    return lax.dot_general(a, b, (dims, ((), ())), preferred_element_type=F32)


def iota(shape, dim):
    return lax.broadcasted_iota(I32, shape, dim)


def one_hot(mask):
    return jnp.where(mask, 1.0, 0.0).astype(BF16)


def gather_kernel(send_hbm, src_hbm, out_hbm, send_ref, src_ref, out_ref, in_sems, out_sems):
    slots, devices = send_ref.shape
    columns, rows = src_ref.shape
    pieces = in_sems.shape[0] - 1
    piece = columns // pieces
    send_copy = pltpu.make_async_copy(send_hbm, send_ref, in_sems.at[pieces])
    send_copy.start()
    copies = []
    for i in range(pieces):
        part = pl.ds(i * piece, piece)
        copies.append(pltpu.make_async_copy(src_hbm.at[part], src_ref.at[part], in_sems.at[i]))
        copies[-1].start()
    send_copy.wait()
    picks = send_ref[...].T
    stride = slots * 5 // 2
    groups = out_sems.shape[0]
    each = devices // groups
    hots = []
    for g in range(groups):
        some = picks[g * each : (g + 1) * each]
        hots.append(
            jnp.concatenate(
                [one_hot(iota((each, rows), 1) == some[:, k : k + 1]) for k in range(slots)], axis=0
            )
        )
    for copy in copies:
        copy.wait()
    high, low = split(src_ref[...])
    copies = []
    for g in range(groups):
        taken = dot(hots[g], high, ((1,), (1,))) + dot(hots[g], low, ((1,), (1,)))
        taken = [taken[k * each : (k + 1) * each] for k in range(slots)]
        base = g * each * stride
        for k in range(slots):
            out_ref[pl.ds(base + k, each, stride=stride), :] = taken[k][:, :LANES]
            out_ref[pl.ds(base + slots + k, each, stride=stride), :] = taken[k][:, LANES : 2 * LANES]
        for k in range(slots // 2):
            both = jnp.concatenate(
                [taken[k][:, 2 * LANES :], taken[k + slots // 2][:, 2 * LANES :]], axis=1
            )
            out_ref[pl.ds(base + 2 * slots + k, each, stride=stride), :] = both
        part = pl.ds(base, each * stride)
        copies.append(pltpu.make_async_copy(out_ref.at[part], out_hbm.at[part], out_sems.at[g]))
        copies[-1].start()
    for copy in copies:
        copy.wait()


def spread_kernel(slots, src_ref, weights_ref, send_ref, spread_ref, place_ref):
    blocks, block_rows, block_cols = weights_ref.shape
    total = spread_ref.shape[2]
    senders = total // slots
    for b in range(blocks):
        slot = src_ref[b : b + 1, :]
        column = (slot % slots) * senders + slot // slots
        hot = one_hot(iota((total, block_cols), 0) == column)
        high, low = split(weights_ref[b])
        summed = dot(high, hot, ((1,), (1,))) + dot(low, hot, ((1,), (1,)))
        high, low = split(summed)
        spread_ref[0, pl.ds(b * block_rows, block_rows), :] = high
        spread_ref[1, pl.ds(b * block_rows, block_rows), :] = low

    slots2, oceans = send_ref.shape
    coupled = blocks * block_rows
    send = send_ref[...]
    ocean, position = jnp.zeros((SUB, coupled), F32), jnp.zeros((SUB, coupled), F32)
    for k in range(slots2):
        hot = one_hot(iota((coupled, oceans), 0) == send[k : k + 1])
        ocean += dot(iota((SUB, oceans), 1).astype(BF16), hot, ((1,), (1,)))
        position += dot(jnp.full((SUB, oceans), k, BF16), hot, ((1,), (1,)))
    real = iota((1, coupled), 1) > 0
    ocean = jnp.where(real, ocean[:1].astype(I32), 0)
    position = jnp.where(real, position[:1].astype(I32), 0)
    half = slots2 // 2
    place_ref[0:1, :] = ocean * (slots2 * 5 // 2) + position
    place_ref[1:2, :] = (position // half) * (oceans * half) + ocean * half + position % half


def couple_kernel(
    slots, slots2, place_any, spread_hbm, recv_ref, out_hbm,
    place_ref, spread_ref, head_high_ref, head_low_ref, out_ref, tail_ref, block_ref, place_sem, spread_sems, out_sems,
):
    place_copy = pltpu.make_async_copy(place_any, place_ref, place_sem)
    place_copy.start()
    _, coupled, total = spread_ref.shape
    blocks = block_ref.shape[0]
    each = coupled // blocks
    spread_copies = []
    for i in range(blocks):
        rows = pl.ds(i * each, each)
        spread_copies.append(
            pltpu.make_async_copy(spread_hbm.at[:, rows], spread_ref.at[:, rows], spread_sems.at[i])
        )
        spread_copies[-1].start()
    senders = total // slots
    stride = slots * 5 // 2
    left = iota((senders, LANES), 1) < HALF
    for k in range(slots):
        rows = pl.ds(k * senders, senders)
        first = recv_ref[pl.ds(k, senders, stride=stride), :]
        second = recv_ref[pl.ds(slots + k, senders, stride=stride), :]
        both = recv_ref[pl.ds(2 * slots + k % (slots // 2), senders, stride=stride), :]
        turned = pltpu.roll(both, HALF, 1)
        third = jnp.where(left, both, turned) if k < slots // 2 else jnp.where(left, turned, both)
        for i, part in enumerate((first, second, third)):
            high, low = split(part)
            head_high_ref[rows, i * LANES : (i + 1) * LANES] = high
            head_low_ref[rows, i * LANES : (i + 1) * LANES] = low
    place_copy.wait()

    wide = slots2 * 5 // 2
    half = slots2 // 2
    oceans = out_ref.shape[0] // wide
    contract = ((1,), (0,))

    def product(i):
        spread_copies[i].wait()
        rows = pl.ds(i * each, each)
        high, low = spread_ref[0, rows], spread_ref[1, rows]
        block_ref[i] = (
            dot(high, head_high_ref[...], contract)
            + dot(high, head_low_ref[...], contract)
            + dot(low, head_high_ref[...], contract)
        )

    def fill(zero):
        first = jnp.broadcast_to(zero[:, :LANES], (slots2, LANES))
        second = jnp.broadcast_to(zero[:, LANES : 2 * LANES], (slots2, LANES))
        third = jnp.broadcast_to(zero[:, 2 * LANES :], (slots2, LANES))

        def step(o, carry):
            base = pl.multiple_of(o * wide, SUB)
            out_ref[pl.ds(base, slots2), :] = first
            out_ref[pl.ds(base + slots2, slots2), :] = second
            tail_ref[pl.ds(pl.multiple_of(o * slots2, slots2), slots2), :] = third
            return carry

        lax.fori_loop(0, oceans, step, 0, unroll=8)

    def scatter(i):
        group = 8
        for base in range(0, each, group):
            rows = range(base, base + group)
            heads = [place_ref[0, i * each + j] for j in rows]
            tails = [place_ref[1, i * each + j] for j in rows]
            values = [[block_ref[i, j : j + 1, c * LANES : (c + 1) * LANES] for c in range(3)] for j in rows]
            for head, tail, value in zip(heads, tails, values):
                out_ref[pl.ds(head, 1), :] = value[0]
                out_ref[pl.ds(head + slots2, 1), :] = value[1]
                tail_ref[pl.ds(tail, 1), :] = value[2]

    product(0)
    fill(block_ref[0, 0:1, :])
    for i in range(1, blocks):
        product(i)
        scatter(i - 1)
    scatter(blocks - 1)

    pieces = out_sems.shape[0]
    some = oceans // pieces
    left = iota((half, LANES), 1) < HALF
    copies = []
    for q in range(pieces):

        def merge(step, carry):
            o = q * some + step
            near = tail_ref[pl.ds(pl.multiple_of(o * half, half), half), :]
            far = tail_ref[pl.ds(pl.multiple_of(oceans * half + o * half, half), half), :]
            out_ref[pl.ds(pl.multiple_of(o * wide + 2 * slots2, SUB), half), :] = jnp.where(left, near, far)
            return carry

        lax.fori_loop(0, some, merge, 0, unroll=8)
        part = pl.ds(q * some * wide, some * wide)
        copies.append(pltpu.make_async_copy(out_ref.at[part], out_hbm.at[part], out_sems.at[q]))
        copies[-1].start()
    for copy in copies:
        copy.wait()


def place_kernel(
    slots2, head_ref, tail_ref, lower_ref, temp_ref, current_ref, arrived_ref, out_hbm, flux_ref, out_ref, sems,
):
    blocks = sems.shape[0]
    columns = out_ref.shape[1]
    row = iota((SUB, LANES), 0)

    def pick(slots):
        value = arrived_ref[pl.ds(slots[0], SUB, stride=0), :]
        for i in range(1, SUB):
            value = jnp.where(row == i, arrived_ref[pl.ds(slots[i], SUB, stride=0), :], value)
        return value

    def block(b):
        base = b * LANES
        if not isinstance(b, int):
            base = pl.multiple_of(base, LANES)
        first, second, third = [], [], []
        for j in range(0, LANES, SUB):
            heads = [head_ref[base + j + i] for i in range(SUB)]
            tails = [tail_ref[base + j + i] for i in range(SUB)]
            first.append(pick(heads))
            second.append(pick([h + slots2 for h in heads]))
            third.append(pick(tails))
        first = jnp.concatenate(first, axis=0).T
        second = jnp.concatenate(second, axis=0).T
        third = jnp.concatenate(third, axis=0).T
        lanes = pl.ds(base, LANES)
        out_ref[b, :LANES, :] = first
        out_ref[b, LANES : 2 * LANES, :] = second
        out_ref[b, 2 * LANES :, :] = jnp.where(lower_ref[:, lanes] > 0, third[:HALF], third[HALF:])
        pltpu.make_async_copy(out_ref.at[b], out_hbm.at[:, lanes], sems.at[b]).start()
        wind_east = first[0:1]
        wind_north = first[LEV : LEV + 1]
        air_temp = first[2 * LEV : 2 * LEV + 1]
        humidity = first[3 * LEV : 3 * LEV + 1]
        surface = temp_ref[:, lanes]
        scale = 0.6 * jnp.sqrt(wind_east * wind_east + wind_north * wind_north + 1.0)
        flux_ref[0:1, lanes] = scale * (air_temp - surface)
        flux_ref[1:2, lanes] = scale * (humidity - 0.5 * jnp.exp(0.2 * surface))
        flux_ref[2:3, lanes] = scale * (wind_east - current_ref[0:1, lanes])
        flux_ref[3:4, lanes] = scale * (wind_north - current_ref[1:2, lanes])

    for b in range(blocks):
        block(b)
    for b in range(blocks):
        pltpu.make_async_copy(out_ref.at[b], out_hbm.at[:, pl.ds(b * LANES, LANES)], sems.at[b]).wait()


def vmem():
    return pl.BlockSpec(memory_space=pltpu.VMEM)


def smem():
    return pl.BlockSpec(memory_space=pltpu.SMEM)


def hbm():
    return pl.BlockSpec(memory_space=pltpu.HBM)


def in_hbm(x):
    return pltpu.with_memory_space_constraint(x, pltpu.HBM)


def params(mib):
    return pltpu.CompilerParams(vmem_limit_bytes=mib * MIB)


def exchange(flat, devices):
    rows = flat.shape[0] // devices
    shaped = flat.reshape(devices, rows // 4, 4, LANES)
    moved = lax.all_to_all(shaped, "comp", split_axis=0, concat_axis=0, tiled=True)
    return moved.reshape(flat.shape)


def shards(
    src_fields, weights, block_src, send_src, coupler_send, ocean_from, surface_temp, ocean_current
):
    devices = lax.axis_size("comp")
    slots, slots2 = send_src.shape[1], coupler_send.shape[1]
    blocks, block_rows, block_cols = weights.shape
    rows, columns = src_fields.shape
    cells = ocean_from.shape[0]
    total = devices * slots
    coupled = blocks * block_rows
    narrow, wide = slots * 5 // 2, slots2 * 5 // 2
    dma = pltpu.SemaphoreType.DMA

    outgoing = pl.pallas_call(
        gather_kernel,
        out_shape=jax.ShapeDtypeStruct((devices * narrow, LANES), F32),
        in_specs=[hbm(), hbm()],
        out_specs=hbm(),
        scratch_shapes=[
            pltpu.VMEM((slots, devices), I32),
            pltpu.VMEM((columns, rows), F32),
            pltpu.VMEM((devices * narrow, LANES), F32),
            dma((5,)),
            dma((4,)),
        ],
        compiler_params=params(16),
        name="gather_rows",
    )(in_hbm(send_src.T), in_hbm(src_fields.T))
    received = exchange(outgoing, devices)

    spread, place = pl.pallas_call(
        lambda *refs: spread_kernel(slots, *refs),
        out_shape=[
            jax.ShapeDtypeStruct((2, coupled, total), BF16),
            jax.ShapeDtypeStruct((2, coupled), I32),
        ],
        in_specs=[vmem(), vmem(), vmem()],
        out_specs=[vmem(), vmem()],
        compiler_params=params(24),
        name="spread_weights",
    )(block_src, weights, coupler_send.T)

    leaving = pl.pallas_call(
        lambda *refs: couple_kernel(slots, slots2, *refs),
        out_shape=jax.ShapeDtypeStruct((devices * wide, LANES), F32),
        in_specs=[vmem(), hbm(), vmem()],
        out_specs=hbm(),
        scratch_shapes=[
            pltpu.SMEM((2, coupled), I32),
            pltpu.VMEM((2, coupled, total), BF16),
            pltpu.VMEM((total, 3 * LANES), BF16),
            pltpu.VMEM((total, 3 * LANES), BF16),
            pltpu.VMEM((devices * wide, LANES), F32),
            pltpu.VMEM((devices * slots2, LANES), F32),
            pltpu.VMEM((4, coupled // 4, 3 * LANES), F32),
            dma(()),
            dma((4,)),
            dma((8,)),
        ],
        compiler_params=params(24),
        name="couple",
    )(place, in_hbm(spread), received)
    arrived = exchange(leaving, devices)

    base = (ocean_from // slots2) * wide
    position = ocean_from % slots2
    half = slots2 // 2
    head = base + position
    tail = base + 2 * slots2 + position % half
    lower = (position < half).astype(I32)[None]
    remapped, fluxes = pl.pallas_call(
        lambda *refs: place_kernel(slots2, *refs),
        out_shape=[jax.ShapeDtypeStruct((columns, cells), F32), jax.ShapeDtypeStruct((4, cells), F32)],
        in_specs=[smem(), smem(), vmem(), vmem(), vmem(), vmem()],
        out_specs=[hbm(), vmem()],
        scratch_shapes=[
            pltpu.VMEM((cells // LANES, columns, LANES), F32),
            dma((cells // LANES,)),
        ],
        compiler_params=params(16),
        name="place",
    )(head, tail, lower, surface_temp[None], ocean_current, arrived)
    return (remapped.T, fluxes)


def solution(mesh):
    return jax.shard_map(
        shards,
        mesh=mesh,
        in_specs=(
            P("comp", None),
            P("comp", None, None),
            P("comp", None),
            P("comp", None),
            P("comp", None),
            P("comp"),
            P("comp"),
            P(None, "comp"),
        ),
        out_specs=(P("comp", None), P(None, "comp")),
        check_vma=False,
    )
```

```python
import jax
import jax.numpy as jnp
from jax import lax
from jax.experimental import pallas as pl
from jax.experimental.pallas import tpu as pltpu
from jax.sharding import PartitionSpec as P

LEV = 8
LANES = 128
HALF = LANES // 2
SUB = 8
BF16 = jnp.bfloat16
F32 = jnp.float32
I32 = jnp.int32
MIB = 1024 * 1024


def split(x):
    high = x.astype(BF16)
    low = (x - high.astype(F32)).astype(BF16)
    return high, low


def dot(a, b, dims):
    return lax.dot_general(a, b, (dims, ((), ())), preferred_element_type=F32)


def iota(shape, dim):
    return lax.broadcasted_iota(I32, shape, dim)


def one_hot(mask):
    return jnp.where(mask, 1.0, 0.0).astype(BF16)


def gather_kernel(send_hbm, src_hbm, out_hbm, send_ref, src_ref, out_ref, in_sems, out_sems):
    slots, devices = send_ref.shape
    columns, rows = src_ref.shape
    pieces = in_sems.shape[0] - 1
    piece = columns // pieces
    send_copy = pltpu.make_async_copy(send_hbm, send_ref, in_sems.at[pieces])
    send_copy.start()
    copies = []
    for i in range(pieces):
        part = pl.ds(i * piece, piece)
        copies.append(pltpu.make_async_copy(src_hbm.at[part], src_ref.at[part], in_sems.at[i]))
        copies[-1].start()
    send_copy.wait()
    picks = send_ref[...].T
    stride = slots * 5 // 2
    groups = out_sems.shape[0]
    each = devices // groups
    hots = []
    for g in range(groups):
        some = picks[g * each : (g + 1) * each]
        hots.append(
            jnp.concatenate(
                [one_hot(iota((each, rows), 1) == some[:, k : k + 1]) for k in range(slots)], axis=0
            )
        )
    for copy in copies:
        copy.wait()
    high, low = split(src_ref[...])
    copies = []
    for g in range(groups):
        taken = dot(hots[g], high, ((1,), (1,))) + dot(hots[g], low, ((1,), (1,)))
        taken = [taken[k * each : (k + 1) * each] for k in range(slots)]
        base = g * each * stride
        for k in range(slots):
            out_ref[pl.ds(base + k, each, stride=stride), :] = taken[k][:, :LANES]
            out_ref[pl.ds(base + slots + k, each, stride=stride), :] = taken[k][:, LANES : 2 * LANES]
        for k in range(slots // 2):
            both = jnp.concatenate(
                [taken[k][:, 2 * LANES :], taken[k + slots // 2][:, 2 * LANES :]], axis=1
            )
            out_ref[pl.ds(base + 2 * slots + k, each, stride=stride), :] = both
        part = pl.ds(base, each * stride)
        copies.append(pltpu.make_async_copy(out_ref.at[part], out_hbm.at[part], out_sems.at[g]))
        copies[-1].start()
    for copy in copies:
        copy.wait()


def spread_kernel(slots, src_ref, weights_ref, send_ref, spread_ref, table_ref, hot_ref):
    blocks, block_rows, block_cols = weights_ref.shape
    _, coupled, kept = spread_ref.shape
    total = hot_ref.shape[1]
    senders = total // slots
    counts = jnp.zeros((SUB, total), F32)
    for b in range(blocks):
        hot_ref[b] = one_hot(iota((total, block_cols), 0) == src_ref[b : b + 1, :])
        counts += dot(jnp.ones((SUB, block_cols), BF16), hot_ref[b], ((1,), (1,)))
    used = counts > 0
    earlier = one_hot(iota((total, total), 0) < iota((total, total), 1))
    rank = dot(one_hot(used), earlier, ((1,), (0,))).astype(I32)
    first_row = iota((SUB, total), 0) == 0
    digits = jnp.where(first_row, rank // 16, rank % 16).astype(BF16)
    for b in range(blocks):
        digit = dot(digits, hot_ref[b], ((1,), (0,))).astype(I32)
        column = digit[0:1] * 16 + digit[1:2]
        hot = one_hot(iota((kept, block_cols), 0) == column)
        high, low = split(weights_ref[b])
        summed = dot(high, hot, ((1,), (1,))) + dot(low, hot, ((1,), (1,)))
        high, low = split(summed)
        spread_ref[0, pl.ds(b * block_rows, block_rows), :] = high
        spread_ref[1, pl.ds(b * block_rows, block_rows), :] = low

    slot = iota((SUB, total), 1)
    digits = jnp.where(first_row, slot // slots, slot % slots).astype(BF16)
    listed = jnp.where(used[:1], rank[:1], -1)
    kept_hot = one_hot(iota((kept, total), 0) == listed)
    digit = dot(digits, kept_hot, ((1,), (1,))).astype(I32)
    sender, k = digit[0:1], digit[1:2]
    half = slots // 2
    table_ref[2:4, :] = jnp.zeros((2, coupled), I32)
    table_ref[2:3, :kept] = sender * (slots * 5 // 2) + k
    table_ref[3:4, :kept] = (k // half) * (half * senders) + (k % half) * senders + sender

    slots2, oceans = send_ref.shape
    send = send_ref[...]
    ocean, position = jnp.zeros((SUB, coupled), F32), jnp.zeros((SUB, coupled), F32)
    for k in range(slots2):
        hot = one_hot(iota((coupled, oceans), 0) == send[k : k + 1])
        ocean += dot(iota((SUB, oceans), 1).astype(BF16), hot, ((1,), (1,)))
        position += dot(jnp.full((SUB, oceans), k, BF16), hot, ((1,), (1,)))
    real = iota((1, coupled), 1) > 0
    ocean = jnp.where(real, ocean[:1].astype(I32), 0)
    position = jnp.where(real, position[:1].astype(I32), 0)
    half = slots2 // 2
    table_ref[0:1, :] = ocean * (2 * slots2) + position
    table_ref[1:2, :] = (position // half) * (oceans * half) + ocean * half + position % half


def couple_kernel(
    slots, slots2, table_any, spread_hbm, recv_ref, out_hbm,
    table_ref, spread_ref, double_ref, rows_ref, rows_high_ref, rows_low_ref,
    head_ref, tail_ref, end_ref, block_ref, end_block_ref, table_sem, spread_sems, head_sems, tail_sems,
):
    table_copy = pltpu.make_async_copy(table_any, table_ref, table_sem)
    table_copy.start()
    _, coupled, kept = spread_ref.shape
    blocks = block_ref.shape[0]
    each = coupled // blocks
    spread_copies = []
    for i in range(blocks):
        rows = pl.ds(i * each, each)
        spread_copies.append(
            pltpu.make_async_copy(spread_hbm.at[:, rows], spread_ref.at[:, rows], spread_sems.at[i])
        )
        spread_copies[-1].start()
    stride = slots * 5 // 2
    senders = recv_ref.shape[0] // stride
    left = iota((senders, LANES), 1) < HALF
    for k in range(slots // 2):
        both = recv_ref[pl.ds(2 * slots + k, senders, stride=stride), :]
        turned = pltpu.roll(both, HALF, 1)
        double_ref[pl.ds(k * senders, senders), :] = jnp.where(left, both, turned)
        double_ref[pl.ds((slots // 2 + k) * senders, senders), :] = jnp.where(left, turned, both)
    table_copy.wait()

    group = 8

    def collect(step, carry):
        base = pl.multiple_of(step * 4 * group, 4 * group)
        for more in range(0, 4 * group, group):
            heads = [table_ref[2, base + more + j] for j in range(group)]
            tails = [table_ref[3, base + more + j] for j in range(group)]
            values = [
                (recv_ref[pl.ds(h, 1), :], recv_ref[pl.ds(h + slots, 1), :], double_ref[pl.ds(t, 1), :])
                for h, t in zip(heads, tails)
            ]
            for j, value in enumerate(values):
                for c in range(3):
                    rows_ref[c, pl.ds(base + more + j, 1), :] = value[c]
        return carry

    lax.fori_loop(0, kept // (4 * group), collect, 0)
    for c in range(3):
        lanes = slice(c * LANES, (c + 1) * LANES)
        rows_high_ref[:, lanes], rows_low_ref[:, lanes] = split(rows_ref[c])

    contract = ((1,), (0,))

    def product(i, lanes):
        rows = pl.ds(i * each, each)
        high, low = spread_ref[0, rows], spread_ref[1, rows]
        return (
            dot(high, rows_high_ref[:, lanes], contract)
            + dot(high, rows_low_ref[:, lanes], contract)
            + dot(low, rows_high_ref[:, lanes], contract)
        )

    oceans = head_ref.shape[0] // (2 * slots2)

    def fill(ref, zero, rows):
        value = jnp.broadcast_to(zero, (rows, LANES))

        def step(o, carry):
            ref[pl.ds(pl.multiple_of(o * rows, rows), rows), :] = value
            return carry

        lax.fori_loop(0, ref.shape[0] // rows, step, 0, unroll=8)

    def fill_pair(first, second):
        first = jnp.broadcast_to(first, (slots2, LANES))
        second = jnp.broadcast_to(second, (slots2, LANES))

        def step(o, carry):
            base = pl.multiple_of(o * 2 * slots2, 2 * slots2)
            head_ref[pl.ds(base, slots2), :] = first
            head_ref[pl.ds(base + slots2, slots2), :] = second
            return carry

        lax.fori_loop(0, oceans, step, 0, unroll=8)

    def scatter(i):
        for base in range(0, each, group):
            rows = range(base, base + group)
            heads = [table_ref[0, i * each + j] for j in rows]
            values = [(block_ref[i, j : j + 1, :LANES], block_ref[i, j : j + 1, LANES:]) for j in rows]
            for head, value in zip(heads, values):
                head_ref[pl.ds(head, 1), :] = value[0]
                head_ref[pl.ds(head + slots2, 1), :] = value[1]

    def scatter_end(i):
        for base in range(0, each, group):
            rows = range(base, base + group)
            tails = [table_ref[1, i * each + j] for j in rows]
            values = [end_block_ref[i, j : j + 1, :] for j in rows]
            for tail, value in zip(tails, values):
                end_ref[pl.ds(tail, 1), :] = value

    head_lanes, tail_lanes = slice(0, 2 * LANES), slice(2 * LANES, 3 * LANES)
    for i in range(blocks):
        spread_copies[i].wait()
        block_ref[i] = product(i, head_lanes)
        if i == 0:
            fill_pair(block_ref[0, 0:1, :LANES], block_ref[0, 0:1, LANES:])
        scatter(i)
    pieces = head_sems.shape[0]
    some = oceans // pieces
    copies = []
    head_view = head_ref.reshape(oceans, 2 * slots2, LANES)
    out_view = out_hbm.reshape(oceans, slots2 * 5 // 2, LANES)
    for q in range(pieces):
        part = pl.ds(q * some, some)
        copies.append(
            pltpu.make_async_copy(head_view.at[part], out_view.at[part, : 2 * slots2], head_sems.at[q])
        )
        copies[-1].start()
    for i in range(blocks):
        end_block_ref[i] = product(i, tail_lanes)
        if i == 0:
            fill(end_ref, end_block_ref[0, 0:1, :], 16)
        scatter_end(i)
    half = slots2 // 2
    left = iota((some * half, LANES), 1) < HALF
    tail_view = tail_ref.reshape(oceans, half, LANES)
    for q in range(pieces):
        rows = pl.ds(q * some * half, some * half)
        far = pl.ds((oceans + q * some) * half, some * half)
        tail_ref[rows] = jnp.where(left, end_ref[rows], end_ref[far])
        part = pl.ds(q * some, some)
        copies.append(
            pltpu.make_async_copy(tail_view.at[part], out_view.at[part, 2 * slots2 :], tail_sems.at[q])
        )
        copies[-1].start()
    for copy in copies:
        copy.wait()


def place_kernel(
    slots2, head_ref, tail_ref, lower_ref, temp_ref, current_ref, arrived_ref, out_hbm, flux_ref, out_ref, sems,
):
    blocks = sems.shape[0]
    columns = out_ref.shape[1]
    row = iota((SUB, LANES), 0)

    def pick(slots):
        value = arrived_ref[pl.ds(slots[0], SUB, stride=0), :]
        for i in range(1, SUB):
            value = jnp.where(row == i, arrived_ref[pl.ds(slots[i], SUB, stride=0), :], value)
        return value

    def block(b):
        base = b * LANES
        if not isinstance(b, int):
            base = pl.multiple_of(base, LANES)
        first, second, third = [], [], []
        for j in range(0, LANES, SUB):
            heads = [head_ref[base + j + i] for i in range(SUB)]
            tails = [tail_ref[base + j + i] for i in range(SUB)]
            first.append(pick(heads))
            second.append(pick([h + slots2 for h in heads]))
            third.append(pick(tails))
        first = jnp.concatenate(first, axis=0).T
        second = jnp.concatenate(second, axis=0).T
        third = jnp.concatenate(third, axis=0).T
        lanes = pl.ds(base, LANES)
        out_ref[b, :LANES, :] = first
        out_ref[b, LANES : 2 * LANES, :] = second
        out_ref[b, 2 * LANES :, :] = jnp.where(lower_ref[:, lanes] > 0, third[:HALF], third[HALF:])
        pltpu.make_async_copy(out_ref.at[b], out_hbm.at[:, lanes], sems.at[b]).start()
        wind_east = first[0:1]
        wind_north = first[LEV : LEV + 1]
        air_temp = first[2 * LEV : 2 * LEV + 1]
        humidity = first[3 * LEV : 3 * LEV + 1]
        surface = temp_ref[:, lanes]
        scale = 0.6 * jnp.sqrt(wind_east * wind_east + wind_north * wind_north + 1.0)
        flux_ref[0:1, lanes] = scale * (air_temp - surface)
        flux_ref[1:2, lanes] = scale * (humidity - 0.5 * jnp.exp(0.2 * surface))
        flux_ref[2:3, lanes] = scale * (wind_east - current_ref[0:1, lanes])
        flux_ref[3:4, lanes] = scale * (wind_north - current_ref[1:2, lanes])

    for b in range(blocks):
        block(b)
    for b in range(blocks):
        pltpu.make_async_copy(out_ref.at[b], out_hbm.at[:, pl.ds(b * LANES, LANES)], sems.at[b]).wait()


def vmem():
    return pl.BlockSpec(memory_space=pltpu.VMEM)


def smem():
    return pl.BlockSpec(memory_space=pltpu.SMEM)


def hbm():
    return pl.BlockSpec(memory_space=pltpu.HBM)


def in_hbm(x):
    return pltpu.with_memory_space_constraint(x, pltpu.HBM)


def params(mib):
    return pltpu.CompilerParams(vmem_limit_bytes=mib * MIB)


def exchange(flat, devices):
    shaped = flat.reshape(devices, flat.shape[0] // devices // 4, 4, LANES)
    moved = lax.all_to_all(shaped, "comp", split_axis=0, concat_axis=0, tiled=True)
    return moved.reshape(flat.shape)


def shards(
    src_fields, weights, block_src, send_src, coupler_send, ocean_from, surface_temp, ocean_current
):
    devices = lax.axis_size("comp")
    slots, slots2 = send_src.shape[1], coupler_send.shape[1]
    blocks, block_rows, block_cols = weights.shape
    rows, columns = src_fields.shape
    cells = ocean_from.shape[0]
    total = devices * slots
    coupled = blocks * block_rows
    narrow, wide = slots * 5 // 2, slots2 * 5 // 2
    dma = pltpu.SemaphoreType.DMA

    outgoing = pl.pallas_call(
        gather_kernel,
        out_shape=jax.ShapeDtypeStruct((devices * narrow, LANES), F32),
        in_specs=[hbm(), hbm()],
        out_specs=hbm(),
        scratch_shapes=[
            pltpu.VMEM((slots, devices), I32),
            pltpu.VMEM((columns, rows), F32),
            pltpu.VMEM((devices * narrow, LANES), F32),
            dma((5,)),
            dma((4,)),
        ],
        compiler_params=params(16),
        name="gather_rows",
    )(in_hbm(send_src.T), in_hbm(src_fields.T))
    received = exchange(outgoing, devices)

    kept = 2 * rows
    spread, table = pl.pallas_call(
        lambda *refs: spread_kernel(slots, *refs),
        out_shape=[
            jax.ShapeDtypeStruct((2, coupled, kept), BF16),
            jax.ShapeDtypeStruct((4, coupled), I32),
        ],
        in_specs=[vmem(), vmem(), vmem()],
        out_specs=[vmem(), vmem()],
        scratch_shapes=[pltpu.VMEM((blocks, total, block_cols), BF16)],
        compiler_params=params(24),
        name="spread_weights",
    )(block_src, weights, coupler_send.T)

    leaving = pl.pallas_call(
        lambda *refs: couple_kernel(slots, slots2, *refs),
        out_shape=jax.ShapeDtypeStruct((devices * wide, LANES), F32),
        in_specs=[vmem(), hbm(), vmem()],
        out_specs=hbm(),
        scratch_shapes=[
            pltpu.SMEM((4, coupled), I32),
            pltpu.VMEM((2, coupled, kept), BF16),
            pltpu.VMEM((devices * slots, LANES), F32),
            pltpu.VMEM((3, kept, LANES), F32),
            pltpu.VMEM((kept, 3 * LANES), BF16),
            pltpu.VMEM((kept, 3 * LANES), BF16),
            pltpu.VMEM((devices * 2 * slots2, LANES), F32),
            pltpu.VMEM((devices * slots2 // 2, LANES), F32),
            pltpu.VMEM((devices * slots2, LANES), F32),
            pltpu.VMEM((4, coupled // 4, 2 * LANES), F32),
            pltpu.VMEM((4, coupled // 4, LANES), F32),
            dma(()),
            dma((4,)),
            dma((4,)),
            dma((4,)),
        ],
        compiler_params=params(51),
        name="couple",
    )(table, in_hbm(spread), received)
    arrived = exchange(leaving, devices)

    base = (ocean_from // slots2) * wide
    position = ocean_from % slots2
    half = slots2 // 2
    head = base + position
    tail = base + 2 * slots2 + position % half
    lower = (position < half).astype(I32)[None]
    remapped, fluxes = pl.pallas_call(
        lambda *refs: place_kernel(slots2, *refs),
        out_shape=[jax.ShapeDtypeStruct((columns, cells), F32), jax.ShapeDtypeStruct((4, cells), F32)],
        in_specs=[smem(), smem(), vmem(), vmem(), vmem(), vmem()],
        out_specs=[hbm(), vmem()],
        scratch_shapes=[
            pltpu.VMEM((cells // LANES, columns, LANES), F32),
            dma((cells // LANES,)),
        ],
        compiler_params=params(16),
        name="place",
    )(head, tail, lower, surface_temp[None], ocean_current, arrived)
    return (remapped.T, fluxes)


def solution(mesh):
    return jax.shard_map(
        shards,
        mesh=mesh,
        in_specs=(
            P("comp", None),
            P("comp", None, None),
            P("comp", None),
            P("comp", None),
            P("comp", None),
            P("comp"),
            P("comp"),
            P(None, "comp"),
        ),
        out_specs=(P("comp", None), P(None, "comp")),
        check_vma=False,
    )
```

```python
import jax
import jax.numpy as jnp
from jax import lax
from jax.experimental import pallas as pl
from jax.experimental.pallas import tpu as pltpu
from jax.sharding import PartitionSpec as P

LEV = 8
LANES = 128
HALF = LANES // 2
SUB = 8
BF16 = jnp.bfloat16
F32 = jnp.float32
I32 = jnp.int32
MIB = 1024 * 1024


def split(x):
    high = x.astype(BF16)
    low = (x - high.astype(F32)).astype(BF16)
    return high, low


def dot(a, b, dims):
    return lax.dot_general(a, b, (dims, ((), ())), preferred_element_type=F32)


def iota(shape, dim):
    return lax.broadcasted_iota(I32, shape, dim)


def one_hot(mask):
    return jnp.where(mask, 1.0, 0.0).astype(BF16)


def gather_kernel(send_hbm, src_hbm, out_hbm, send_ref, src_ref, out_ref, in_sems, out_sems):
    slots, devices = send_ref.shape
    columns, rows = src_ref.shape
    pieces = in_sems.shape[0] - 1
    piece = columns // pieces
    send_copy = pltpu.make_async_copy(send_hbm, send_ref, in_sems.at[pieces])
    send_copy.start()
    copies = []
    for i in range(pieces):
        part = pl.ds(i * piece, piece)
        copies.append(pltpu.make_async_copy(src_hbm.at[part], src_ref.at[part], in_sems.at[i]))
        copies[-1].start()
    send_copy.wait()
    picks = send_ref[...].T
    stride = slots * 5 // 2
    groups = out_sems.shape[0]
    each = devices // groups
    hots = []
    for g in range(groups):
        some = picks[g * each : (g + 1) * each]
        hots.append(
            jnp.concatenate(
                [one_hot(iota((each, rows), 1) == some[:, k : k + 1]) for k in range(slots)], axis=0
            )
        )
    for copy in copies:
        copy.wait()
    high, low = split(src_ref[...])
    copies = []
    for g in range(groups):
        taken = dot(hots[g], high, ((1,), (1,))) + dot(hots[g], low, ((1,), (1,)))
        taken = [taken[k * each : (k + 1) * each] for k in range(slots)]
        base = g * each * stride
        for k in range(slots):
            out_ref[pl.ds(base + k, each, stride=stride), :] = taken[k][:, :LANES]
            out_ref[pl.ds(base + slots + k, each, stride=stride), :] = taken[k][:, LANES : 2 * LANES]
        for k in range(slots // 2):
            both = jnp.concatenate(
                [taken[k][:, 2 * LANES :], taken[k + slots // 2][:, 2 * LANES :]], axis=1
            )
            out_ref[pl.ds(base + 2 * slots + k, each, stride=stride), :] = both
        part = pl.ds(base, each * stride)
        copies.append(pltpu.make_async_copy(out_ref.at[part], out_hbm.at[part], out_sems.at[g]))
        copies[-1].start()
    for copy in copies:
        copy.wait()


def spread_kernel(slots, src_ref, weights_ref, send_ref, spread_ref, take_ref, table_ref, hot_ref):
    blocks, block_rows, block_cols = weights_ref.shape
    coupled, kept = spread_ref.shape[0], spread_ref.shape[1] // 2
    total = hot_ref.shape[1]
    senders = total // slots
    counts = jnp.zeros((SUB, total), F32)
    for b in range(blocks):
        hot_ref[b] = one_hot(iota((total, block_cols), 0) == src_ref[b : b + 1, :])
        counts += dot(jnp.ones((SUB, block_cols), BF16), hot_ref[b], ((1,), (1,)))
    used = counts > 0
    earlier = one_hot(iota((total, total), 0) < iota((total, total), 1))
    rank = dot(one_hot(used), earlier, ((1,), (0,))).astype(I32)
    first_row = iota((SUB, total), 0) == 0
    digits = jnp.where(first_row, rank // 16, rank % 16).astype(BF16)
    for b in range(blocks):
        digit = dot(digits, hot_ref[b], ((1,), (0,))).astype(I32)
        column = digit[0:1] * 16 + digit[1:2]
        hot = one_hot(iota((kept, block_cols), 0) == column)
        high, low = split(weights_ref[b])
        summed = dot(high, hot, ((1,), (1,))) + dot(low, hot, ((1,), (1,)))
        high, low = split(summed)
        spread_ref[pl.ds(b * block_rows, block_rows), :kept] = high
        spread_ref[pl.ds(b * block_rows, block_rows), kept:] = low

    slot = iota((SUB, total), 1)
    digits = jnp.where(first_row, slot // slots, slot % slots).astype(BF16)
    listed = jnp.where(used[:1], rank[:1], -1)
    kept_hot = one_hot(iota((kept, total), 0) == listed)
    digit = dot(digits, kept_hot, ((1,), (1,))).astype(I32)
    sender, k = digit[0:1], digit[1:2]
    half = slots // 2
    take_ref[0:1, :] = sender * (slots * 5 // 2) + k
    take_ref[1:2, :] = (k // half) * (half * senders) + (k % half) * senders + sender

    slots2, oceans = send_ref.shape
    send = send_ref[...]
    ocean, position = jnp.zeros((SUB, coupled), F32), jnp.zeros((SUB, coupled), F32)
    for k in range(slots2):
        hot = one_hot(iota((coupled, oceans), 0) == send[k : k + 1])
        ocean += dot(iota((SUB, oceans), 1).astype(BF16), hot, ((1,), (1,)))
        position += dot(jnp.full((SUB, oceans), k, BF16), hot, ((1,), (1,)))
    real = iota((1, coupled), 1) > 0
    ocean = jnp.where(real, ocean[:1].astype(I32), 0)
    position = jnp.where(real, position[:1].astype(I32), 0)
    half = slots2 // 2
    table_ref[0:1, :] = ocean * (2 * slots2) + position
    table_ref[1:2, :] = (position // half) * (oceans * half) + ocean * half + position % half


def couple_kernel(
    slots, slots2, take_any, table_any, spread_hbm, recv_ref, out_hbm,
    take_ref, table_ref, spread_ref, double_ref, rows_ref, rows_high_ref, rows_low_ref,
    head_ref, tail_ref, end_ref, block_ref, end_block_ref, table_sems, spread_sems, head_sems, tail_sems,
):
    coupled, kept = spread_ref.shape[0], spread_ref.shape[1] // 2
    take_copy = pltpu.make_async_copy(take_any, take_ref, table_sems.at[0])
    take_copy.start()
    table_copy = pltpu.make_async_copy(table_any, table_ref, table_sems.at[1])
    table_copy.start()
    blocks = block_ref.shape[0]
    each = coupled // blocks
    spread_copies = []
    for i in range(blocks):
        rows = pl.ds(i * each, each)
        spread_copies.append(
            pltpu.make_async_copy(spread_hbm.at[rows], spread_ref.at[rows], spread_sems.at[i])
        )
        spread_copies[-1].start()
    stride = slots * 5 // 2
    senders = recv_ref.shape[0] // stride
    left = iota((senders, LANES), 1) < HALF
    for k in range(slots // 2):
        both = recv_ref[pl.ds(2 * slots + k, senders, stride=stride), :]
        turned = pltpu.roll(both, HALF, 1)
        double_ref[pl.ds(k * senders, senders), :] = jnp.where(left, both, turned)
        double_ref[pl.ds((slots // 2 + k) * senders, senders), :] = jnp.where(left, turned, both)
    take_copy.wait()

    group = 8

    for base in range(0, kept, group):
        rows = range(base, base + group)
        heads = [take_ref[0, j] for j in rows]
        tails = [take_ref[1, j] for j in rows]
        values = [
            (recv_ref[pl.ds(h, 1), :], recv_ref[pl.ds(h + slots, 1), :], double_ref[pl.ds(t, 1), :])
            for h, t in zip(heads, tails)
        ]
        for j, value in zip(rows, values):
            for c in range(3):
                rows_ref[c, j : j + 1, :] = value[c]
    for c in range(3):
        lanes = slice(c * LANES, (c + 1) * LANES)
        high, low = split(rows_ref[c])
        rows_high_ref[:kept, lanes] = high
        rows_high_ref[kept:, lanes] = high
        rows_low_ref[:, lanes] = low

    contract = ((1,), (0,))

    def product(i, lanes):
        rows = pl.ds(i * each, each)
        return dot(spread_ref[rows], rows_high_ref[:, lanes], contract) + dot(
            spread_ref[rows, :kept], rows_low_ref[:, lanes], contract
        )

    oceans = head_ref.shape[0] // (2 * slots2)

    def scatter(i):
        for base in range(0, each, group):
            rows = range(base, base + group)
            heads = [table_ref[0, i * each + j] for j in rows]
            values = [(block_ref[i, j : j + 1, :LANES], block_ref[i, j : j + 1, LANES:]) for j in rows]
            for head, value in zip(heads, values):
                head_ref[pl.ds(head, 1), :] = value[0]
                head_ref[pl.ds(head + slots2, 1), :] = value[1]

    def scatter_end(i):
        for base in range(0, each, group):
            rows = range(base, base + group)
            tails = [table_ref[1, i * each + j] for j in rows]
            values = [end_block_ref[i, j : j + 1, :] for j in rows]
            for tail, value in zip(tails, values):
                end_ref[pl.ds(tail, 1), :] = value

    head_lanes, tail_lanes = slice(0, 2 * LANES), slice(2 * LANES, 3 * LANES)
    table_copy.wait()
    for copy in spread_copies:
        copy.wait()
    for i in range(blocks):
        block_ref[i] = product(i, head_lanes)
    first = jnp.broadcast_to(block_ref[0, 0:1, :LANES], (slots2, LANES))
    second = jnp.broadcast_to(block_ref[0, 0:1, LANES:], (slots2, LANES))
    for o in range(oceans):
        head_ref[2 * o * slots2 : (2 * o + 1) * slots2, :] = first
        head_ref[(2 * o + 1) * slots2 : (2 * o + 2) * slots2, :] = second
    for i in range(blocks):
        scatter(i)
    pieces = head_sems.shape[0]
    some = oceans // pieces
    copies = []
    head_view = head_ref.reshape(oceans, 2 * slots2, LANES)
    out_view = out_hbm.reshape(oceans, slots2 * 5 // 2, LANES)
    for q in range(pieces):
        part = pl.ds(q * some, some)
        copies.append(
            pltpu.make_async_copy(head_view.at[part], out_view.at[part, : 2 * slots2], head_sems.at[q])
        )
        copies[-1].start()
    for i in range(blocks):
        end_block_ref[i] = product(i, tail_lanes)
    end_ref[...] = jnp.broadcast_to(end_block_ref[0, 0:1, :], end_ref.shape)
    for i in range(blocks):
        scatter_end(i)
    half = slots2 // 2
    left = iota((some * half, LANES), 1) < HALF
    tail_view = tail_ref.reshape(oceans, half, LANES)
    for q in range(pieces):
        rows = pl.ds(q * some * half, some * half)
        far = pl.ds((oceans + q * some) * half, some * half)
        tail_ref[rows] = jnp.where(left, end_ref[rows], end_ref[far])
        part = pl.ds(q * some, some)
        copies.append(
            pltpu.make_async_copy(tail_view.at[part], out_view.at[part, 2 * slots2 :], tail_sems.at[q])
        )
        copies[-1].start()
    for copy in copies:
        copy.wait()


def place_kernel(
    slots2, slot_ref, lower_ref, temp_ref, current_ref, arrived_ref, out_hbm, flux_hbm,
    out_ref, flux_ref, sems,
):
    blocks = sems.shape[0] - 1
    row = iota((SUB, LANES), 0)

    def pick(slots):
        value = arrived_ref[pl.ds(slots[0], SUB, stride=0), :]
        for i in range(1, SUB):
            value = jnp.where(row == i, arrived_ref[pl.ds(slots[i], SUB, stride=0), :], value)
        return value

    def block(b):
        base = b * LANES
        first, second, third = [], [], []
        for j in range(base, base + LANES, SUB):
            heads = [slot_ref[0, j + i] for i in range(SUB)]
            tails = [slot_ref[1, j + i] for i in range(SUB)]
            first.append(pick(heads))
            second.append(pick([h + slots2 for h in heads]))
            third.append(pick(tails))
        first, second, third = (jnp.concatenate(x, axis=0).T for x in (first, second, third))
        lanes = pl.ds(base, LANES)
        out_ref[b, :LANES, :] = first
        out_ref[b, LANES : 2 * LANES, :] = second
        out_ref[b, 2 * LANES :, :] = jnp.where(lower_ref[:, lanes] > 0, third[:HALF], third[HALF:])
        wind_east = first[0:1]
        wind_north = first[LEV : LEV + 1]
        air_temp = first[2 * LEV : 2 * LEV + 1]
        humidity = first[3 * LEV : 3 * LEV + 1]
        surface = temp_ref[:, lanes]
        scale = 0.6 * jnp.sqrt(wind_east * wind_east + wind_north * wind_north + 1.0)
        flux_ref[0:1, lanes] = scale * (air_temp - surface)
        flux_ref[1:2, lanes] = scale * (humidity - 0.5 * jnp.exp(0.2 * surface))
        flux_ref[2:3, lanes] = scale * (wind_east - current_ref[0:1, lanes])
        flux_ref[3:4, lanes] = scale * (wind_north - current_ref[1:2, lanes])

    copies = []
    phases = 2
    for phase in range(phases):
        some = range(phase * blocks // phases, (phase + 1) * blocks // phases)
        for b in some:
            block(b)
        for b in some:
            lanes = pl.ds(b * LANES, LANES)
            copies.append(pltpu.make_async_copy(out_ref.at[b], out_hbm.at[:, lanes], sems.at[b]))
            copies[-1].start()
    copies.append(pltpu.make_async_copy(flux_ref, flux_hbm, sems.at[blocks]))
    copies[-1].start()
    for copy in copies:
        copy.wait()


def vmem():
    return pl.BlockSpec(memory_space=pltpu.VMEM)


def smem():
    return pl.BlockSpec(memory_space=pltpu.SMEM)


def hbm():
    return pl.BlockSpec(memory_space=pltpu.HBM)


def in_hbm(x):
    return pltpu.with_memory_space_constraint(x, pltpu.HBM)


def params(mib):
    return pltpu.CompilerParams(vmem_limit_bytes=mib * MIB)


def exchange(flat, devices):
    shaped = flat.reshape(devices, flat.shape[0] // devices // 4, 4, LANES)
    moved = lax.all_to_all(shaped, "comp", split_axis=0, concat_axis=0, tiled=True)
    return moved.reshape(flat.shape)


def shards(
    src_fields, weights, block_src, send_src, coupler_send, ocean_from, surface_temp, ocean_current
):
    devices = lax.axis_size("comp")
    slots, slots2 = send_src.shape[1], coupler_send.shape[1]
    blocks, block_rows, block_cols = weights.shape
    rows, columns = src_fields.shape
    cells = ocean_from.shape[0]
    total = devices * slots
    coupled = blocks * block_rows
    narrow, wide = slots * 5 // 2, slots2 * 5 // 2
    dma = pltpu.SemaphoreType.DMA

    outgoing = pl.pallas_call(
        gather_kernel,
        out_shape=jax.ShapeDtypeStruct((devices * narrow, LANES), F32),
        in_specs=[hbm(), hbm()],
        out_specs=hbm(),
        scratch_shapes=[
            pltpu.VMEM((slots, devices), I32),
            pltpu.VMEM((columns, rows), F32),
            pltpu.VMEM((devices * narrow, LANES), F32),
            dma((5,)),
            dma((4,)),
        ],
        compiler_params=params(16),
        name="gather_rows",
    )(in_hbm(send_src.T), in_hbm(src_fields.T))
    received = exchange(outgoing, devices)

    kept = 2 * rows
    spread, take, table = pl.pallas_call(
        lambda *refs: spread_kernel(slots, *refs),
        out_shape=[
            jax.ShapeDtypeStruct((coupled, 2 * kept), BF16),
            jax.ShapeDtypeStruct((2, kept), I32),
            jax.ShapeDtypeStruct((2, coupled), I32),
        ],
        in_specs=[vmem(), vmem(), vmem()],
        out_specs=[vmem(), vmem(), vmem()],
        scratch_shapes=[pltpu.VMEM((blocks, total, block_cols), BF16)],
        compiler_params=params(24),
        name="spread_weights",
    )(block_src, weights, coupler_send.T)

    leaving = pl.pallas_call(
        lambda *refs: couple_kernel(slots, slots2, *refs),
        out_shape=jax.ShapeDtypeStruct((devices * wide, LANES), F32),
        in_specs=[vmem(), vmem(), hbm(), vmem()],
        out_specs=hbm(),
        scratch_shapes=[
            pltpu.SMEM((2, kept), I32),
            pltpu.SMEM((2, coupled), I32),
            pltpu.VMEM((coupled, 2 * kept), BF16),
            pltpu.VMEM((devices * slots, LANES), F32),
            pltpu.VMEM((3, kept, LANES), F32),
            pltpu.VMEM((2 * kept, 3 * LANES), BF16),
            pltpu.VMEM((kept, 3 * LANES), BF16),
            pltpu.VMEM((devices * 2 * slots2, LANES), F32),
            pltpu.VMEM((devices * slots2 // 2, LANES), F32),
            pltpu.VMEM((devices * slots2, LANES), F32),
            pltpu.VMEM((2, coupled // 2, 2 * LANES), F32),
            pltpu.VMEM((2, coupled // 2, LANES), F32),
            dma((2,)),
            dma((2,)),
            dma((4,)),
            dma((4,)),
        ],
        compiler_params=params(51),
        name="couple",
    )(take, table, in_hbm(spread), received)
    arrived = exchange(leaving, devices)

    base = (ocean_from // slots2) * wide
    position = ocean_from % slots2
    half = slots2 // 2
    head = base + position
    tail = base + 2 * slots2 + position % half
    lower = (position < half).astype(I32)[None]
    remapped, fluxes = pl.pallas_call(
        lambda *refs: place_kernel(slots2, *refs),
        out_shape=[jax.ShapeDtypeStruct((columns, cells), F32), jax.ShapeDtypeStruct((4, cells), F32)],
        in_specs=[smem(), vmem(), vmem(), vmem(), vmem()],
        out_specs=[hbm(), hbm()],
        scratch_shapes=[
            pltpu.VMEM((cells // LANES, columns, LANES), F32),
            pltpu.VMEM((4, cells), F32),
            dma((cells // LANES + 1,)),
        ],
        compiler_params=params(16),
        name="place",
    )(jnp.stack([head, tail]), lower, surface_temp[None], ocean_current, arrived)
    return (remapped.T, fluxes)


def solution(mesh):
    return jax.shard_map(
        shards,
        mesh=mesh,
        in_specs=(
            P("comp", None),
            P("comp", None, None),
            P("comp", None),
            P("comp", None),
            P("comp", None),
            P("comp"),
            P("comp"),
            P(None, "comp"),
        ),
        out_specs=(P("comp", None), P(None, "comp")),
        check_vma=False,
    )
```

```python
import jax
import jax.numpy as jnp
from jax import lax
from jax.experimental import pallas as pl
from jax.experimental.pallas import tpu as pltpu
from jax.sharding import PartitionSpec as P

LEV = 8
LANES = 128
HALF = LANES // 2
SUB = 8
BF16 = jnp.bfloat16
F32 = jnp.float32
I32 = jnp.int32
MIB = 1024 * 1024


def split(x):
    high = x.astype(BF16)
    low = (x - high.astype(F32)).astype(BF16)
    return high, low


def dot(a, b, dims):
    return lax.dot_general(a, b, (dims, ((), ())), preferred_element_type=F32)


def iota(shape, dim):
    return lax.broadcasted_iota(I32, shape, dim)


def one_hot(mask):
    return jnp.where(mask, 1.0, 0.0).astype(BF16)


def gather_kernel(send_hbm, src_hbm, out_hbm, send_ref, src_ref, out_ref, in_sems, out_sems):
    slots, devices = send_ref.shape
    columns, rows = src_ref.shape
    pieces = in_sems.shape[0] - 1
    piece = columns // pieces
    send_copy = pltpu.make_async_copy(send_hbm, send_ref, in_sems.at[pieces])
    send_copy.start()
    copies = []
    for i in range(pieces):
        part = pl.ds(i * piece, piece)
        copies.append(pltpu.make_async_copy(src_hbm.at[part], src_ref.at[part], in_sems.at[i]))
        copies[-1].start()
    send_copy.wait()
    picks = send_ref[...].T
    stride = slots * 5 // 2
    groups = out_sems.shape[0]
    each = devices // groups
    hots = []
    for g in range(groups):
        some = picks[g * each : (g + 1) * each]
        hots.append(
            jnp.concatenate(
                [one_hot(iota((each, rows), 1) == some[:, k : k + 1]) for k in range(slots)], axis=0
            )
        )
    for copy in copies:
        copy.wait()
    high, low = split(src_ref[...])
    copies = []
    for g in range(groups):
        taken = dot(hots[g], high, ((1,), (1,))) + dot(hots[g], low, ((1,), (1,)))
        taken = [taken[k * each : (k + 1) * each] for k in range(slots)]
        base = g * each * stride
        for k in range(slots):
            out_ref[pl.ds(base + k, each, stride=stride), :] = taken[k][:, :LANES]
            out_ref[pl.ds(base + slots + k, each, stride=stride), :] = taken[k][:, LANES : 2 * LANES]
        for k in range(slots // 2):
            both = jnp.concatenate(
                [taken[k][:, 2 * LANES :], taken[k + slots // 2][:, 2 * LANES :]], axis=1
            )
            out_ref[pl.ds(base + 2 * slots + k, each, stride=stride), :] = both
        part = pl.ds(base, each * stride)
        copies.append(pltpu.make_async_copy(out_ref.at[part], out_hbm.at[part], out_sems.at[g]))
        copies[-1].start()
    for copy in copies:
        copy.wait()


def spread_kernel(slots, src_ref, weights_ref, send_ref, spread_ref, take_ref, table_ref, hot_ref):
    blocks, block_rows, block_cols = weights_ref.shape
    coupled, kept = spread_ref.shape[0], spread_ref.shape[1] // 3
    total = hot_ref.shape[1]
    senders = total // slots
    counts = jnp.zeros((SUB, total), F32)
    for b in range(blocks):
        hot_ref[b] = one_hot(iota((total, block_cols), 0) == src_ref[b : b + 1, :])
        counts += dot(jnp.ones((SUB, block_cols), BF16), hot_ref[b], ((1,), (1,)))
    used = counts > 0
    earlier = one_hot(iota((total, total), 0) < iota((total, total), 1))
    rank = dot(one_hot(used), earlier, ((1,), (0,))).astype(I32)
    first_row = iota((SUB, total), 0) == 0
    digits = jnp.where(first_row, rank // 16, rank % 16).astype(BF16)
    for b in range(blocks):
        digit = dot(digits, hot_ref[b], ((1,), (0,))).astype(I32)
        column = digit[0:1] * 16 + digit[1:2]
        hot = one_hot(iota((kept, block_cols), 0) == column)
        high, low = split(weights_ref[b])
        summed = dot(high, hot, ((1,), (1,))) + dot(low, hot, ((1,), (1,)))
        high, low = split(summed)
        for i, part in enumerate((high, low, high)):
            spread_ref[b * block_rows : (b + 1) * block_rows, i * kept : (i + 1) * kept] = part

    slot = iota((SUB, total), 1)
    digits = jnp.where(first_row, slot // slots, slot % slots).astype(BF16)
    listed = jnp.where(used[:1], rank[:1], -1)
    kept_hot = one_hot(iota((kept, total), 0) == listed)
    digit = dot(digits, kept_hot, ((1,), (1,))).astype(I32)
    sender, k = digit[0:1], digit[1:2]
    half = slots // 2
    take_ref[0:1, :] = sender * (slots * 5 // 2) + k
    take_ref[1:2, :] = (k // half) * (half * senders) + (k % half) * senders + sender

    slots2, oceans = send_ref.shape
    send = send_ref[...]
    ocean, position = jnp.zeros((SUB, coupled), F32), jnp.zeros((SUB, coupled), F32)
    for k in range(slots2):
        hot = one_hot(iota((coupled, oceans), 0) == send[k : k + 1])
        ocean += dot(iota((SUB, oceans), 1).astype(BF16), hot, ((1,), (1,)))
        position += dot(jnp.full((SUB, oceans), k, BF16), hot, ((1,), (1,)))
    real = iota((1, coupled), 1) > 0
    ocean = jnp.where(real, ocean[:1].astype(I32), 0)
    position = jnp.where(real, position[:1].astype(I32), 0)
    half = slots2 // 2
    table_ref[0:1, :] = ocean * (2 * slots2) + position
    table_ref[1:2, :] = (position // half) * (oceans * half) + ocean * half + position % half


def couple_kernel(
    slots, slots2, take_any, table_any, spread_ref, recv_ref, out_hbm,
    take_ref, table_ref, double_ref, stacked_ref,
    head_ref, tail_ref, end_ref, block_ref, end_block_ref, table_sems, head_sems, tail_sems,
):
    coupled, kept = spread_ref.shape[0], spread_ref.shape[1] // 3
    take_copy = pltpu.make_async_copy(take_any, take_ref, table_sems.at[0])
    take_copy.start()
    table_copy = pltpu.make_async_copy(table_any, table_ref, table_sems.at[1])
    table_copy.start()
    blocks = block_ref.shape[0]
    each = coupled // blocks
    stride = slots * 5 // 2
    senders = recv_ref.shape[0] // stride
    left = iota((senders, LANES), 1) < HALF
    for k in range(slots // 2):
        both = recv_ref[pl.ds(2 * slots + k, senders, stride=stride), :]
        turned = pltpu.roll(both, HALF, 1)
        double_ref[pl.ds(k * senders, senders), :] = jnp.where(left, both, turned)
        double_ref[pl.ds((slots // 2 + k) * senders, senders), :] = jnp.where(left, turned, both)
    take_copy.wait()

    group = 4
    row = iota((SUB, LANES), 0)

    def pick(ref, slots):
        value = ref[pl.ds(slots[0], SUB, stride=0), :]
        for i in range(1, SUB):
            value = jnp.where(row == i, ref[pl.ds(slots[i], SUB, stride=0), :], value)
        return value

    for base in range(0, kept, 2 * SUB):
        parts = []
        for start in (base, base + SUB):
            heads = [take_ref[0, j] for j in range(start, start + SUB)]
            tails = [take_ref[1, j] for j in range(start, start + SUB)]
            parts.append(
                (pick(recv_ref, heads), pick(recv_ref, [h + slots for h in heads]), pick(double_ref, tails))
            )
        for c in range(3):
            lanes = slice(c * LANES, (c + 1) * LANES)
            high, low = split(jnp.concatenate([parts[0][c], parts[1][c]], axis=0))
            for i, part in enumerate((high, high, low)):
                stacked_ref[i * kept + base : i * kept + base + 2 * SUB, lanes] = part

    contract = ((1,), (0,))

    def product(i, lanes):
        rows = pl.ds(i * each, each)
        return dot(spread_ref[rows], stacked_ref[:, lanes], contract)

    oceans = head_ref.shape[0] // (2 * slots2)

    def scatter(i):
        for base in range(0, each, group):
            rows = range(base, base + group)
            heads = [table_ref[0, i * each + j] for j in rows]
            values = [(block_ref[i, j : j + 1, :LANES], block_ref[i, j : j + 1, LANES:]) for j in rows]
            for head, value in zip(heads, values):
                head_ref[pl.ds(head, 1), :] = value[0]
                head_ref[pl.ds(head + slots2, 1), :] = value[1]

    def scatter_end(i):
        for base in range(0, each, group):
            rows = range(base, base + group)
            tails = [table_ref[1, i * each + j] for j in rows]
            values = [end_block_ref[i, j : j + 1, :] for j in rows]
            for tail, value in zip(tails, values):
                end_ref[pl.ds(tail, 1), :] = value

    head_lanes, tail_lanes = slice(0, 2 * LANES), slice(2 * LANES, 3 * LANES)
    table_copy.wait()
    for i in range(blocks):
        block_ref[i] = product(i, head_lanes)
        if i == 0:
            first = jnp.broadcast_to(block_ref[0, 0:1, :LANES], (slots2, LANES))
            second = jnp.broadcast_to(block_ref[0, 0:1, LANES:], (slots2, LANES))
            for o in range(oceans):
                head_ref[2 * o * slots2 : (2 * o + 1) * slots2, :] = first
                head_ref[(2 * o + 1) * slots2 : (2 * o + 2) * slots2, :] = second
        else:
            scatter(i - 1)
    scatter(blocks - 1)
    pieces = head_sems.shape[0]
    some = oceans // pieces
    copies = []
    head_view = head_ref.reshape(oceans, 2 * slots2, LANES)
    out_view = out_hbm.reshape(oceans, slots2 * 5 // 2, LANES)
    for q in range(pieces):
        part = pl.ds(q * some, some)
        copies.append(
            pltpu.make_async_copy(head_view.at[part], out_view.at[part, : 2 * slots2], head_sems.at[q])
        )
        copies[-1].start()
    for i in range(blocks):
        end_block_ref[i] = product(i, tail_lanes)
        if i == 0:
            end_ref[...] = jnp.broadcast_to(end_block_ref[0, 0:1, :], end_ref.shape)
        else:
            scatter_end(i - 1)
    scatter_end(blocks - 1)
    half = slots2 // 2
    left = iota((some * half, LANES), 1) < HALF
    tail_view = tail_ref.reshape(oceans, half, LANES)
    for q in range(pieces):
        rows = pl.ds(q * some * half, some * half)
        far = pl.ds((oceans + q * some) * half, some * half)
        tail_ref[rows] = jnp.where(left, end_ref[rows], end_ref[far])
        part = pl.ds(q * some, some)
        copies.append(
            pltpu.make_async_copy(tail_view.at[part], out_view.at[part, 2 * slots2 :], tail_sems.at[q])
        )
        copies[-1].start()
    for copy in copies:
        copy.wait()


def place_kernel(
    slots2, slot_ref, lower_ref, temp_ref, current_ref, arrived_ref, out_hbm, flux_hbm,
    out_ref, flux_ref, sems,
):
    blocks = sems.shape[0] - 1
    row = iota((SUB, LANES), 0)

    def pick(slots):
        value = arrived_ref[pl.ds(slots[0], SUB, stride=0), :]
        for i in range(1, SUB):
            value = jnp.where(row == i, arrived_ref[pl.ds(slots[i], SUB, stride=0), :], value)
        return value

    def block(b):
        base = b * LANES
        first, second, third = [], [], []
        for j in range(base, base + LANES, SUB):
            heads = [slot_ref[0, j + i] for i in range(SUB)]
            tails = [slot_ref[1, j + i] for i in range(SUB)]
            first.append(pick(heads))
            second.append(pick([h + slots2 for h in heads]))
            third.append(pick(tails))
        first, second, third = (jnp.concatenate(x, axis=0).T for x in (first, second, third))
        lanes = pl.ds(base, LANES)
        out_ref[b, :LANES, :] = first
        out_ref[b, LANES : 2 * LANES, :] = second
        out_ref[b, 2 * LANES :, :] = jnp.where(lower_ref[:, lanes] > 0, third[:HALF], third[HALF:])
        wind_east = first[0:1]
        wind_north = first[LEV : LEV + 1]
        air_temp = first[2 * LEV : 2 * LEV + 1]
        humidity = first[3 * LEV : 3 * LEV + 1]
        surface = temp_ref[:, lanes]
        scale = 0.6 * jnp.sqrt(wind_east * wind_east + wind_north * wind_north + 1.0)
        flux_ref[0:1, lanes] = scale * (air_temp - surface)
        flux_ref[1:2, lanes] = scale * (humidity - 0.5 * jnp.exp(0.2 * surface))
        flux_ref[2:3, lanes] = scale * (wind_east - current_ref[0:1, lanes])
        flux_ref[3:4, lanes] = scale * (wind_north - current_ref[1:2, lanes])

    copies = []
    phases = 2
    for phase in range(phases):
        some = range(phase * blocks // phases, (phase + 1) * blocks // phases)
        for b in some:
            block(b)
        for b in some:
            lanes = pl.ds(b * LANES, LANES)
            copies.append(pltpu.make_async_copy(out_ref.at[b], out_hbm.at[:, lanes], sems.at[b]))
            copies[-1].start()
    copies.append(pltpu.make_async_copy(flux_ref, flux_hbm, sems.at[blocks]))
    copies[-1].start()
    for copy in copies:
        copy.wait()


def vmem():
    return pl.BlockSpec(memory_space=pltpu.VMEM)


def smem():
    return pl.BlockSpec(memory_space=pltpu.SMEM)


def hbm():
    return pl.BlockSpec(memory_space=pltpu.HBM)


def in_hbm(x):
    return pltpu.with_memory_space_constraint(x, pltpu.HBM)


def params(mib):
    return pltpu.CompilerParams(vmem_limit_bytes=mib * MIB)


def exchange(flat, devices):
    shaped = flat.reshape(devices, flat.shape[0] // devices // 4, 4, LANES)
    moved = lax.all_to_all(shaped, "comp", split_axis=0, concat_axis=0, tiled=True)
    return moved.reshape(flat.shape)


def shards(
    src_fields, weights, block_src, send_src, coupler_send, ocean_from, surface_temp, ocean_current
):
    devices = lax.axis_size("comp")
    slots, slots2 = send_src.shape[1], coupler_send.shape[1]
    blocks, block_rows, block_cols = weights.shape
    rows, columns = src_fields.shape
    cells = ocean_from.shape[0]
    total = devices * slots
    coupled = blocks * block_rows
    narrow, wide = slots * 5 // 2, slots2 * 5 // 2
    dma = pltpu.SemaphoreType.DMA

    outgoing = pl.pallas_call(
        gather_kernel,
        out_shape=jax.ShapeDtypeStruct((devices * narrow, LANES), F32),
        in_specs=[hbm(), hbm()],
        out_specs=hbm(),
        scratch_shapes=[
            pltpu.VMEM((slots, devices), I32),
            pltpu.VMEM((columns, rows), F32),
            pltpu.VMEM((devices * narrow, LANES), F32),
            dma((5,)),
            dma((4,)),
        ],
        compiler_params=params(16),
        name="gather_rows",
    )(in_hbm(send_src.T), in_hbm(src_fields.T))
    received = exchange(outgoing, devices)

    kept = 2 * rows
    spread, take, table = pl.pallas_call(
        lambda *refs: spread_kernel(slots, *refs),
        out_shape=[
            jax.ShapeDtypeStruct((coupled, 3 * kept), BF16),
            jax.ShapeDtypeStruct((2, kept), I32),
            jax.ShapeDtypeStruct((2, coupled), I32),
        ],
        in_specs=[vmem(), vmem(), vmem()],
        out_specs=[vmem(), vmem(), vmem()],
        scratch_shapes=[pltpu.VMEM((blocks, total, block_cols), BF16)],
        compiler_params=params(24),
        name="spread_weights",
    )(block_src, weights, coupler_send.T)

    leaving = pl.pallas_call(
        lambda *refs: couple_kernel(slots, slots2, *refs),
        out_shape=jax.ShapeDtypeStruct((devices * wide, LANES), F32),
        in_specs=[vmem(), vmem(), vmem(), vmem()],
        out_specs=hbm(),
        scratch_shapes=[
            pltpu.SMEM((2, kept), I32),
            pltpu.SMEM((2, coupled), I32),
            pltpu.VMEM((devices * slots, LANES), F32),
            pltpu.VMEM((3 * kept, 3 * LANES), BF16),
            pltpu.VMEM((devices * 2 * slots2, LANES), F32),
            pltpu.VMEM((devices * slots2 // 2, LANES), F32),
            pltpu.VMEM((devices * slots2, LANES), F32),
            pltpu.VMEM((8, coupled // 8, 2 * LANES), F32),
            pltpu.VMEM((8, coupled // 8, LANES), F32),
            dma((2,)),
            dma((4,)),
            dma((4,)),
        ],
        compiler_params=params(24),
        name="couple",
    )(take, table, spread, received)
    arrived = exchange(leaving, devices)

    base = (ocean_from // slots2) * wide
    position = ocean_from % slots2
    half = slots2 // 2
    head = base + position
    tail = base + 2 * slots2 + position % half
    lower = (position < half).astype(I32)[None]
    remapped, fluxes = pl.pallas_call(
        lambda *refs: place_kernel(slots2, *refs),
        out_shape=[jax.ShapeDtypeStruct((columns, cells), F32), jax.ShapeDtypeStruct((4, cells), F32)],
        in_specs=[smem(), vmem(), vmem(), vmem(), vmem()],
        out_specs=[hbm(), hbm()],
        scratch_shapes=[
            pltpu.VMEM((cells // LANES, columns, LANES), F32),
            pltpu.VMEM((4, cells), F32),
            dma((cells // LANES + 1,)),
        ],
        compiler_params=params(16),
        name="place",
    )(jnp.stack([head, tail]), lower, surface_temp[None], ocean_current, arrived)
    return (remapped.T, fluxes)


def solution(mesh):
    return jax.shard_map(
        shards,
        mesh=mesh,
        in_specs=(
            P("comp", None),
            P("comp", None, None),
            P("comp", None),
            P("comp", None),
            P("comp", None),
            P("comp"),
            P("comp"),
            P(None, "comp"),
        ),
        out_specs=(P("comp", None), P(None, "comp")),
        check_vma=False,
    )
```

```python
import jax
import jax.numpy as jnp
from jax import lax
from jax.experimental import pallas as pl
from jax.experimental.pallas import tpu as pltpu
from jax.sharding import PartitionSpec as P

LEV = 8
LANES = 128
HALF = LANES // 2
SUB = 8
BF16 = jnp.bfloat16
F32 = jnp.float32
I32 = jnp.int32
MIB = 1024 * 1024


def split(x):
    high = x.astype(BF16)
    low = (x - high.astype(F32)).astype(BF16)
    return high, low


def dot(a, b, dims):
    return lax.dot_general(a, b, (dims, ((), ())), preferred_element_type=F32)


def iota(shape, dim):
    return lax.broadcasted_iota(I32, shape, dim)


def one_hot(mask):
    return jnp.where(mask, 1.0, 0.0).astype(BF16)


def gather_kernel(send_hbm, src_hbm, out_hbm, send_ref, src_ref, out_ref, in_sems, out_sems):
    slots, devices = send_ref.shape
    columns, rows = src_ref.shape
    pieces = in_sems.shape[0] - 1
    piece = columns // pieces
    send_copy = pltpu.make_async_copy(send_hbm, send_ref, in_sems.at[pieces])
    send_copy.start()
    copies = []
    for i in range(pieces):
        part = pl.ds(i * piece, piece)
        copies.append(pltpu.make_async_copy(src_hbm.at[part], src_ref.at[part], in_sems.at[i]))
        copies[-1].start()
    send_copy.wait()
    picks = send_ref[...].T
    stride = slots * 5 // 2
    groups = out_sems.shape[0]
    each = devices // groups
    hots = []
    for g in range(groups):
        some = picks[g * each : (g + 1) * each]
        hots.append(
            jnp.concatenate(
                [one_hot(iota((each, rows), 1) == some[:, k : k + 1]) for k in range(slots)], axis=0
            )
        )
    for copy in copies:
        copy.wait()
    high, low = split(src_ref[...])
    copies = []
    for g in range(groups):
        taken = dot(hots[g], high, ((1,), (1,))) + dot(hots[g], low, ((1,), (1,)))
        taken = [taken[k * each : (k + 1) * each] for k in range(slots)]
        base = g * each * stride
        for k in range(slots):
            out_ref[pl.ds(base + k, each, stride=stride), :] = taken[k][:, :LANES]
            out_ref[pl.ds(base + slots + k, each, stride=stride), :] = taken[k][:, LANES : 2 * LANES]
        for k in range(slots // 2):
            both = jnp.concatenate(
                [taken[k][:, 2 * LANES :], taken[k + slots // 2][:, 2 * LANES :]], axis=1
            )
            out_ref[pl.ds(base + 2 * slots + k, each, stride=stride), :] = both
        part = pl.ds(base, each * stride)
        copies.append(pltpu.make_async_copy(out_ref.at[part], out_hbm.at[part], out_sems.at[g]))
        copies[-1].start()
    for copy in copies:
        copy.wait()


def spread_kernel(slots, src_ref, weights_ref, send_ref, spread_ref, take_ref, table_ref, hot_ref):
    blocks, block_rows, block_cols = weights_ref.shape
    coupled, kept = spread_ref.shape[0], spread_ref.shape[1] // 2
    total = hot_ref.shape[1]
    senders = total // slots
    counts = jnp.zeros((SUB, total), F32)
    for b in range(blocks):
        hot_ref[b] = one_hot(iota((total, block_cols), 0) == src_ref[b : b + 1, :])
        counts += dot(jnp.ones((SUB, block_cols), BF16), hot_ref[b], ((1,), (1,)))
    used = counts > 0
    earlier = one_hot(iota((total, total), 0) < iota((total, total), 1))
    rank = dot(one_hot(used), earlier, ((1,), (0,))).astype(I32)
    first_row = iota((SUB, total), 0) == 0
    digits = jnp.where(first_row, rank // 16, rank % 16).astype(BF16)
    for b in range(blocks):
        digit = dot(digits, hot_ref[b], ((1,), (0,))).astype(I32)
        column = digit[0:1] * 16 + digit[1:2]
        hot = one_hot(iota((kept, block_cols), 0) == column)
        high, low = split(weights_ref[b])
        summed = dot(high, hot, ((1,), (1,))) + dot(low, hot, ((1,), (1,)))
        high, low = split(summed)
        for i, part in enumerate((high, low)):
            spread_ref[b * block_rows : (b + 1) * block_rows, i * kept : (i + 1) * kept] = part

    slot = iota((SUB, total), 1)
    digits = jnp.where(first_row, slot // slots, slot % slots).astype(BF16)
    listed = jnp.where(used[:1], rank[:1], -1)
    kept_hot = one_hot(iota((kept, total), 0) == listed)
    digit = dot(digits, kept_hot, ((1,), (1,))).astype(I32)
    sender, k = digit[0:1], digit[1:2]
    half = slots // 2
    take_ref[0:1, :] = sender * (slots * 5 // 2) + k
    take_ref[1:2, :] = (k // half) * (half * senders) + (k % half) * senders + sender

    slots2, oceans = send_ref.shape
    send = send_ref[...]
    ocean, position = jnp.zeros((SUB, coupled), F32), jnp.zeros((SUB, coupled), F32)
    for k in range(slots2):
        hot = one_hot(iota((coupled, oceans), 0) == send[k : k + 1])
        ocean += dot(iota((SUB, oceans), 1).astype(BF16), hot, ((1,), (1,)))
        position += dot(jnp.full((SUB, oceans), k, BF16), hot, ((1,), (1,)))
    real = iota((1, coupled), 1) > 0
    ocean = jnp.where(real, ocean[:1].astype(I32), 0)
    position = jnp.where(real, position[:1].astype(I32), 0)
    half = slots2 // 2
    table_ref[0:1, :] = ocean * (2 * slots2) + position
    table_ref[1:2, :] = (position // half) * (oceans * half) + ocean * half + position % half


def couple_kernel(
    slots, slots2, take_any, table_any, spread_ref, recv_ref, out_hbm,
    take_ref, table_ref, double_ref, stacked_ref,
    head_ref, tail_ref, end_ref, block_ref, end_block_ref, table_sems, head_sems, tail_sems,
):
    coupled, kept = spread_ref.shape[0], spread_ref.shape[1] // 2
    take_copy = pltpu.make_async_copy(take_any, take_ref, table_sems.at[0])
    take_copy.start()
    table_copy = pltpu.make_async_copy(table_any, table_ref, table_sems.at[1])
    table_copy.start()
    blocks = block_ref.shape[0]
    each = coupled // blocks
    stride = slots * 5 // 2
    senders = recv_ref.shape[0] // stride
    left = iota((senders, LANES), 1) < HALF
    for k in range(slots // 2):
        both = recv_ref[pl.ds(2 * slots + k, senders, stride=stride), :]
        turned = pltpu.roll(both, HALF, 1)
        double_ref[pl.ds(k * senders, senders), :] = jnp.where(left, both, turned)
        double_ref[pl.ds((slots // 2 + k) * senders, senders), :] = jnp.where(left, turned, both)
    take_copy.wait()

    group = 4
    row = iota((SUB, LANES), 0)

    def pick(ref, slots):
        value = ref[pl.ds(slots[0], SUB, stride=0), :]
        for i in range(1, SUB):
            value = jnp.where(row == i, ref[pl.ds(slots[i], SUB, stride=0), :], value)
        return value

    for base in range(0, kept, 2 * SUB):
        parts = []
        for start in (base, base + SUB):
            heads = [take_ref[0, j] for j in range(start, start + SUB)]
            tails = [take_ref[1, j] for j in range(start, start + SUB)]
            parts.append(
                (pick(recv_ref, heads), pick(recv_ref, [h + slots for h in heads]), pick(double_ref, tails))
            )
        for c in range(3):
            lanes = slice(c * LANES, (c + 1) * LANES)
            high, low = split(jnp.concatenate([parts[0][c], parts[1][c]], axis=0))
            for i, part in enumerate((high, high, low)):
                stacked_ref[i * kept + base : i * kept + base + 2 * SUB, lanes] = part

    contract = ((1,), (0,))

    def product(i, lanes):
        rows = pl.ds(i * each, each)
        return dot(spread_ref[rows], stacked_ref[: 2 * kept, lanes], contract) + dot(
            spread_ref[rows, :kept], stacked_ref[2 * kept :, lanes], contract
        )

    oceans = head_ref.shape[0] // (2 * slots2)

    def scatter(i):
        for base in range(0, each, group):
            rows = range(base, base + group)
            heads = [table_ref[0, i * each + j] for j in rows]
            values = [(block_ref[i, j : j + 1, :LANES], block_ref[i, j : j + 1, LANES:]) for j in rows]
            for head, value in zip(heads, values):
                head_ref[pl.ds(head, 1), :] = value[0]
                head_ref[pl.ds(head + slots2, 1), :] = value[1]

    def scatter_end(i):
        for base in range(0, each, group):
            rows = range(base, base + group)
            tails = [table_ref[1, i * each + j] for j in rows]
            values = [end_block_ref[i, j : j + 1, :] for j in rows]
            for tail, value in zip(tails, values):
                end_ref[pl.ds(tail, 1), :] = value

    head_lanes, tail_lanes = slice(0, 2 * LANES), slice(2 * LANES, 3 * LANES)
    table_copy.wait()
    for i in range(blocks):
        block_ref[i] = product(i, head_lanes)
        if i == 0:
            first = jnp.broadcast_to(block_ref[0, 0:1, :LANES], (slots2, LANES))
            second = jnp.broadcast_to(block_ref[0, 0:1, LANES:], (slots2, LANES))
            for o in range(oceans):
                head_ref[2 * o * slots2 : (2 * o + 1) * slots2, :] = first
                head_ref[(2 * o + 1) * slots2 : (2 * o + 2) * slots2, :] = second
        else:
            scatter(i - 1)
    scatter(blocks - 1)
    pieces = head_sems.shape[0]
    some = oceans // pieces
    copies = []
    head_view = head_ref.reshape(oceans, 2 * slots2, LANES)
    out_view = out_hbm.reshape(oceans, slots2 * 5 // 2, LANES)
    for q in range(pieces):
        part = pl.ds(q * some, some)
        copies.append(
            pltpu.make_async_copy(head_view.at[part], out_view.at[part, : 2 * slots2], head_sems.at[q])
        )
        copies[-1].start()
    for i in range(blocks):
        end_block_ref[i] = product(i, tail_lanes)
        if i == 0:
            end_ref[...] = jnp.broadcast_to(end_block_ref[0, 0:1, :], end_ref.shape)
        else:
            scatter_end(i - 1)
    scatter_end(blocks - 1)
    half = slots2 // 2
    left = iota((some * half, LANES), 1) < HALF
    tail_view = tail_ref.reshape(oceans, half, LANES)
    for q in range(pieces):
        rows = pl.ds(q * some * half, some * half)
        far = pl.ds((oceans + q * some) * half, some * half)
        tail_ref[rows] = jnp.where(left, end_ref[rows], end_ref[far])
        part = pl.ds(q * some, some)
        copies.append(
            pltpu.make_async_copy(tail_view.at[part], out_view.at[part, 2 * slots2 :], tail_sems.at[q])
        )
        copies[-1].start()
    for copy in copies:
        copy.wait()


def place_kernel(
    slots2, slot_ref, lower_ref, temp_ref, current_ref, arrived_ref, out_hbm, flux_hbm,
    out_ref, flux_ref, sems,
):
    blocks = sems.shape[0] - 1
    row = iota((SUB, LANES), 0)

    def pick(slots):
        value = arrived_ref[pl.ds(slots[0], SUB, stride=0), :]
        for i in range(1, SUB):
            value = jnp.where(row == i, arrived_ref[pl.ds(slots[i], SUB, stride=0), :], value)
        return value

    def block(b):
        base = b * LANES
        first, second, third = [], [], []
        for j in range(base, base + LANES, SUB):
            heads = [slot_ref[0, j + i] for i in range(SUB)]
            tails = [slot_ref[1, j + i] for i in range(SUB)]
            first.append(pick(heads))
            second.append(pick([h + slots2 for h in heads]))
            third.append(pick(tails))
        first, second, third = (jnp.concatenate(x, axis=0).T for x in (first, second, third))
        lanes = pl.ds(base, LANES)
        out_ref[b, :LANES, :] = first
        out_ref[b, LANES : 2 * LANES, :] = second
        out_ref[b, 2 * LANES :, :] = jnp.where(lower_ref[:, lanes] > 0, third[:HALF], third[HALF:])
        wind_east = first[0:1]
        wind_north = first[LEV : LEV + 1]
        air_temp = first[2 * LEV : 2 * LEV + 1]
        humidity = first[3 * LEV : 3 * LEV + 1]
        surface = temp_ref[:, lanes]
        scale = 0.6 * jnp.sqrt(wind_east * wind_east + wind_north * wind_north + 1.0)
        flux_ref[0:1, lanes] = scale * (air_temp - surface)
        flux_ref[1:2, lanes] = scale * (humidity - 0.5 * jnp.exp(0.2 * surface))
        flux_ref[2:3, lanes] = scale * (wind_east - current_ref[0:1, lanes])
        flux_ref[3:4, lanes] = scale * (wind_north - current_ref[1:2, lanes])

    copies = []
    phases = 2
    for phase in range(phases):
        some = range(phase * blocks // phases, (phase + 1) * blocks // phases)
        for b in some:
            block(b)
        for b in some:
            lanes = pl.ds(b * LANES, LANES)
            copies.append(pltpu.make_async_copy(out_ref.at[b], out_hbm.at[:, lanes], sems.at[b]))
            copies[-1].start()
    copies.append(pltpu.make_async_copy(flux_ref, flux_hbm, sems.at[blocks]))
    copies[-1].start()
    for copy in copies:
        copy.wait()


def vmem():
    return pl.BlockSpec(memory_space=pltpu.VMEM)


def smem():
    return pl.BlockSpec(memory_space=pltpu.SMEM)


def hbm():
    return pl.BlockSpec(memory_space=pltpu.HBM)


def in_hbm(x):
    return pltpu.with_memory_space_constraint(x, pltpu.HBM)


def params(mib):
    return pltpu.CompilerParams(vmem_limit_bytes=mib * MIB)


def exchange(flat, devices):
    shaped = flat.reshape(devices, flat.shape[0] // devices // 4, 4, LANES)
    moved = lax.all_to_all(shaped, "comp", split_axis=0, concat_axis=0, tiled=True)
    return moved.reshape(flat.shape)


def shards(
    src_fields, weights, block_src, send_src, coupler_send, ocean_from, surface_temp, ocean_current
):
    devices = lax.axis_size("comp")
    slots, slots2 = send_src.shape[1], coupler_send.shape[1]
    blocks, block_rows, block_cols = weights.shape
    rows, columns = src_fields.shape
    cells = ocean_from.shape[0]
    total = devices * slots
    coupled = blocks * block_rows
    narrow, wide = slots * 5 // 2, slots2 * 5 // 2
    dma = pltpu.SemaphoreType.DMA

    outgoing = pl.pallas_call(
        gather_kernel,
        out_shape=jax.ShapeDtypeStruct((devices * narrow, LANES), F32),
        in_specs=[hbm(), hbm()],
        out_specs=hbm(),
        scratch_shapes=[
            pltpu.VMEM((slots, devices), I32),
            pltpu.VMEM((columns, rows), F32),
            pltpu.VMEM((devices * narrow, LANES), F32),
            dma((5,)),
            dma((4,)),
        ],
        compiler_params=params(16),
        name="gather_rows",
    )(in_hbm(send_src.T), in_hbm(src_fields.T))
    received = exchange(outgoing, devices)

    kept = 2 * rows
    spread, take, table = pl.pallas_call(
        lambda *refs: spread_kernel(slots, *refs),
        out_shape=[
            jax.ShapeDtypeStruct((coupled, 2 * kept), BF16),
            jax.ShapeDtypeStruct((2, kept), I32),
            jax.ShapeDtypeStruct((2, coupled), I32),
        ],
        in_specs=[vmem(), vmem(), vmem()],
        out_specs=[vmem(), vmem(), vmem()],
        scratch_shapes=[pltpu.VMEM((blocks, total, block_cols), BF16)],
        compiler_params=params(24),
        name="spread_weights",
    )(block_src, weights, coupler_send.T)

    leaving = pl.pallas_call(
        lambda *refs: couple_kernel(slots, slots2, *refs),
        out_shape=jax.ShapeDtypeStruct((devices * wide, LANES), F32),
        in_specs=[vmem(), vmem(), vmem(), vmem()],
        out_specs=hbm(),
        scratch_shapes=[
            pltpu.SMEM((2, kept), I32),
            pltpu.SMEM((2, coupled), I32),
            pltpu.VMEM((devices * slots, LANES), F32),
            pltpu.VMEM((3 * kept, 3 * LANES), BF16),
            pltpu.VMEM((devices * 2 * slots2, LANES), F32),
            pltpu.VMEM((devices * slots2 // 2, LANES), F32),
            pltpu.VMEM((devices * slots2, LANES), F32),
            pltpu.VMEM((8, coupled // 8, 2 * LANES), F32),
            pltpu.VMEM((8, coupled // 8, LANES), F32),
            dma((2,)),
            dma((4,)),
            dma((4,)),
        ],
        compiler_params=params(24),
        name="couple",
    )(take, table, spread, received)
    arrived = exchange(leaving, devices)

    base = (ocean_from // slots2) * wide
    position = ocean_from % slots2
    half = slots2 // 2
    head = base + position
    tail = base + 2 * slots2 + position % half
    lower = (position < half).astype(I32)[None]
    remapped, fluxes = pl.pallas_call(
        lambda *refs: place_kernel(slots2, *refs),
        out_shape=[jax.ShapeDtypeStruct((columns, cells), F32), jax.ShapeDtypeStruct((4, cells), F32)],
        in_specs=[smem(), vmem(), vmem(), vmem(), vmem()],
        out_specs=[hbm(), hbm()],
        scratch_shapes=[
            pltpu.VMEM((cells // LANES, columns, LANES), F32),
            pltpu.VMEM((4, cells), F32),
            dma((cells // LANES + 1,)),
        ],
        compiler_params=params(16),
        name="place",
    )(jnp.stack([head, tail]), lower, surface_temp[None], ocean_current, arrived)
    return (remapped.T, fluxes)


def solution(mesh):
    return jax.shard_map(
        shards,
        mesh=mesh,
        in_specs=(
            P("comp", None),
            P("comp", None, None),
            P("comp", None),
            P("comp", None),
            P("comp", None),
            P("comp"),
            P("comp"),
            P(None, "comp"),
        ),
        out_specs=(P("comp", None), P(None, "comp")),
        check_vma=False,
    )
```

```python
import jax
import jax.numpy as jnp
from jax import lax
from jax.experimental import pallas as pl
from jax.experimental.pallas import tpu as pltpu
from jax.sharding import PartitionSpec as P

LEV = 8
LANES = 128
HALF = LANES // 2
SUB = 8
BF16 = jnp.bfloat16
F32 = jnp.float32
I32 = jnp.int32
MIB = 1024 * 1024


def split(x):
    high = x.astype(BF16)
    low = (x - high.astype(F32)).astype(BF16)
    return high, low


def dot(a, b, dims):
    return lax.dot_general(a, b, (dims, ((), ())), preferred_element_type=F32)


def iota(shape, dim):
    return lax.broadcasted_iota(I32, shape, dim)


def one_hot(mask):
    return jnp.where(mask, 1.0, 0.0).astype(BF16)


def gather_kernel(send_hbm, src_hbm, out_hbm, send_ref, src_ref, out_ref, in_sems, out_sems):
    slots, devices = send_ref.shape
    columns, rows = src_ref.shape
    pieces = in_sems.shape[0] - 1
    piece = columns // pieces
    send_copy = pltpu.make_async_copy(send_hbm, send_ref, in_sems.at[pieces])
    send_copy.start()
    copies = []
    for i in range(pieces):
        part = pl.ds(i * piece, piece)
        copies.append(pltpu.make_async_copy(src_hbm.at[part], src_ref.at[part], in_sems.at[i]))
        copies[-1].start()
    send_copy.wait()
    picks = send_ref[...].T
    stride = slots * 5 // 2
    groups = out_sems.shape[0]
    each = devices // groups
    hots = []
    for g in range(groups):
        some = picks[g * each : (g + 1) * each]
        hots.append(
            jnp.concatenate(
                [one_hot(iota((each, rows), 1) == some[:, k : k + 1]) for k in range(slots)], axis=0
            )
        )
    for copy in copies:
        copy.wait()
    high, low = split(src_ref[...])
    copies = []
    for g in range(groups):
        taken = dot(hots[g], high, ((1,), (1,))) + dot(hots[g], low, ((1,), (1,)))
        taken = [taken[k * each : (k + 1) * each] for k in range(slots)]
        base = g * each * stride
        for k in range(slots):
            out_ref[pl.ds(base + k, each, stride=stride), :] = taken[k][:, :LANES]
            out_ref[pl.ds(base + slots + k, each, stride=stride), :] = taken[k][:, LANES : 2 * LANES]
        for k in range(slots // 2):
            both = jnp.concatenate(
                [taken[k][:, 2 * LANES :], taken[k + slots // 2][:, 2 * LANES :]], axis=1
            )
            out_ref[pl.ds(base + 2 * slots + k, each, stride=stride), :] = both
        part = pl.ds(base, each * stride)
        copies.append(pltpu.make_async_copy(out_ref.at[part], out_hbm.at[part], out_sems.at[g]))
        copies[-1].start()
    for copy in copies:
        copy.wait()


def spread_kernel(slots, src_ref, weights_ref, send_ref, spread_ref, take_ref, table_ref, hot_ref):
    blocks, block_rows, block_cols = weights_ref.shape
    coupled, kept = spread_ref.shape[0], spread_ref.shape[1] // 2
    total = hot_ref.shape[1]
    senders = total // slots
    counts = jnp.zeros((SUB, total), F32)
    for b in range(blocks):
        hot_ref[b] = one_hot(iota((total, block_cols), 0) == src_ref[b : b + 1, :])
        counts += dot(jnp.ones((SUB, block_cols), BF16), hot_ref[b], ((1,), (1,)))
    used = counts > 0
    earlier = one_hot(iota((total, total), 0) < iota((total, total), 1))
    rank = dot(one_hot(used), earlier, ((1,), (0,))).astype(I32)
    first_row = iota((SUB, total), 0) == 0
    digits = jnp.where(first_row, rank // 16, rank % 16).astype(BF16)
    for b in range(blocks):
        digit = dot(digits, hot_ref[b], ((1,), (0,))).astype(I32)
        column = digit[0:1] * 16 + digit[1:2]
        hot = one_hot(iota((kept, block_cols), 0) == column)
        high, low = split(weights_ref[b])
        summed = dot(high, hot, ((1,), (1,))) + dot(low, hot, ((1,), (1,)))
        high, low = split(summed)
        for i, part in enumerate((high, low)):
            spread_ref[b * block_rows : (b + 1) * block_rows, i * kept : (i + 1) * kept] = part

    slot = iota((SUB, total), 1)
    digits = jnp.where(first_row, slot // slots, slot % slots).astype(BF16)
    listed = jnp.where(used[:1], rank[:1], -1)
    kept_hot = one_hot(iota((kept, total), 0) == listed)
    digit = dot(digits, kept_hot, ((1,), (1,))).astype(I32)
    sender, k = digit[0:1], digit[1:2]
    half = slots // 2
    take_ref[0:1, :] = sender * (slots * 5 // 2) + k
    take_ref[1:2, :] = (k // half) * (half * senders) + (k % half) * senders + sender

    slots2, oceans = send_ref.shape
    send = send_ref[...]
    ocean, position = jnp.zeros((SUB, coupled), F32), jnp.zeros((SUB, coupled), F32)
    for k in range(slots2):
        hot = one_hot(iota((coupled, oceans), 0) == send[k : k + 1])
        ocean += dot(iota((SUB, oceans), 1).astype(BF16), hot, ((1,), (1,)))
        position += dot(jnp.full((SUB, oceans), k, BF16), hot, ((1,), (1,)))
    real = iota((1, coupled), 1) > 0
    ocean = jnp.where(real, ocean[:1].astype(I32), 0)
    position = jnp.where(real, position[:1].astype(I32), 0)
    half = slots2 // 2
    table_ref[0:1, :] = ocean * (2 * slots2) + position
    table_ref[1:2, :] = (position // half) * (oceans * half) + ocean * half + position % half


def couple_kernel(
    slots, slots2, take_any, table_any, spread_ref, recv_ref, out_hbm,
    take_ref, table_ref, double_ref, stacked_ref,
    head_ref, tail_ref, end_ref, block_ref, end_block_ref, table_sems, head_sems, tail_sems,
):
    coupled, kept = spread_ref.shape[0], spread_ref.shape[1] // 2
    take_copy = pltpu.make_async_copy(take_any, take_ref, table_sems.at[0])
    take_copy.start()
    table_copy = pltpu.make_async_copy(table_any, table_ref, table_sems.at[1])
    table_copy.start()
    blocks = block_ref.shape[0]
    each = coupled // blocks
    stride = slots * 5 // 2
    senders = recv_ref.shape[0] // stride
    left = iota((senders, LANES), 1) < HALF
    for k in range(slots // 2):
        both = recv_ref[pl.ds(2 * slots + k, senders, stride=stride), :]
        turned = pltpu.roll(both, HALF, 1)
        double_ref[pl.ds(k * senders, senders), :] = jnp.where(left, both, turned)
        double_ref[pl.ds((slots // 2 + k) * senders, senders), :] = jnp.where(left, turned, both)
    take_copy.wait()

    group = 4
    row = iota((SUB, LANES), 0)

    def pick(ref, slots):
        value = ref[pl.ds(slots[0], SUB, stride=0), :]
        for i in range(1, SUB):
            value = jnp.where(row == i, ref[pl.ds(slots[i], SUB, stride=0), :], value)
        return value

    for base in range(0, kept, 2 * SUB):
        parts = []
        for start in (base, base + SUB):
            heads = [take_ref[0, j] for j in range(start, start + SUB)]
            tails = [take_ref[1, j] for j in range(start, start + SUB)]
            parts.append(
                (pick(recv_ref, heads), pick(recv_ref, [h + slots for h in heads]), pick(double_ref, tails))
            )
        for c in range(3):
            lanes = slice(c * LANES, (c + 1) * LANES)
            high, low = split(jnp.concatenate([parts[0][c], parts[1][c]], axis=0))
            for i, part in enumerate((high, high, low)):
                stacked_ref[i * kept + base : i * kept + base + 2 * SUB, lanes] = part

    contract = ((1,), (0,))

    def product(i, lanes):
        rows = pl.ds(i * each, each)
        return dot(spread_ref[rows], stacked_ref[: 2 * kept, lanes], contract) + dot(
            spread_ref[rows, :kept], stacked_ref[2 * kept :, lanes], contract
        )

    oceans = head_ref.shape[0] // (2 * slots2)

    def scatter(i):
        for base in range(0, each, group):
            rows = range(base, base + group)
            heads = [table_ref[0, i * each + j] for j in rows]
            values = [(block_ref[i, j : j + 1, :LANES], block_ref[i, j : j + 1, LANES:]) for j in rows]
            for head, value in zip(heads, values):
                head_ref[pl.ds(head, 1), :] = value[0]
                head_ref[pl.ds(head + slots2, 1), :] = value[1]

    def scatter_end(i):
        for base in range(0, each, group):
            rows = range(base, base + group)
            tails = [table_ref[1, i * each + j] for j in rows]
            values = [end_block_ref[i, j : j + 1, :] for j in rows]
            for tail, value in zip(tails, values):
                end_ref[pl.ds(tail, 1), :] = value

    head_lanes, tail_lanes = slice(0, 2 * LANES), slice(2 * LANES, 3 * LANES)
    table_copy.wait()
    for i in range(blocks):
        block_ref[i] = product(i, head_lanes)
        if i == 0:
            first = jnp.broadcast_to(block_ref[0, 0:1, :LANES], (slots2, LANES))
            second = jnp.broadcast_to(block_ref[0, 0:1, LANES:], (slots2, LANES))
            for o in range(oceans):
                head_ref[2 * o * slots2 : (2 * o + 1) * slots2, :] = first
                head_ref[(2 * o + 1) * slots2 : (2 * o + 2) * slots2, :] = second
        else:
            scatter(i - 1)
    scatter(blocks - 1)
    pieces = head_sems.shape[0]
    some = oceans // pieces
    copies = []
    head_view = head_ref.reshape(oceans, 2 * slots2, LANES)
    out_view = out_hbm.reshape(oceans, slots2 * 5 // 2, LANES)
    for q in range(pieces):
        part = pl.ds(q * some, some)
        copies.append(
            pltpu.make_async_copy(head_view.at[part], out_view.at[part, : 2 * slots2], head_sems.at[q])
        )
        copies[-1].start()
    for i in range(blocks):
        end_block_ref[i] = product(i, tail_lanes)
        if i == 0:
            end_ref[...] = jnp.broadcast_to(end_block_ref[0, 0:1, :], end_ref.shape)
        else:
            scatter_end(i - 1)
    scatter_end(blocks - 1)
    half = slots2 // 2
    left = iota((some * half, LANES), 1) < HALF
    tail_view = tail_ref.reshape(oceans, half, LANES)
    for q in range(pieces):
        rows = pl.ds(q * some * half, some * half)
        far = pl.ds((oceans + q * some) * half, some * half)
        tail_ref[rows] = jnp.where(left, end_ref[rows], end_ref[far])
        part = pl.ds(q * some, some)
        copies.append(
            pltpu.make_async_copy(tail_view.at[part], out_view.at[part, 2 * slots2 :], tail_sems.at[q])
        )
        copies[-1].start()
    for copy in copies:
        copy.wait()


def place_kernel(
    slots2, slot_ref, lower_ref, temp_ref, current_ref, arrived_ref, out_hbm, flux_hbm,
    out_ref, flux_ref, sems,
):
    blocks = sems.shape[0] - 1
    row = iota((SUB, LANES), 0)

    def pick(slots):
        value = arrived_ref[pl.ds(slots[0], SUB, stride=0), :]
        for i in range(1, SUB):
            value = jnp.where(row == i, arrived_ref[pl.ds(slots[i], SUB, stride=0), :], value)
        return value

    def block(b):
        base = b * LANES
        first, second, third = [], [], []
        for j in range(base, base + LANES, SUB):
            heads = [slot_ref[0, j + i] for i in range(SUB)]
            tails = [slot_ref[1, j + i] for i in range(SUB)]
            first.append(pick(heads))
            second.append(pick([h + slots2 for h in heads]))
            third.append(pick(tails))
        first, second, third = (jnp.concatenate(x, axis=0).T for x in (first, second, third))
        lanes = pl.ds(base, LANES)
        out_ref[b, :LANES, :] = first
        out_ref[b, LANES : 2 * LANES, :] = second
        out_ref[b, 2 * LANES :, :] = jnp.where(lower_ref[:, lanes] > 0, third[:HALF], third[HALF:])
        wind_east = first[0:1]
        wind_north = first[LEV : LEV + 1]
        air_temp = first[2 * LEV : 2 * LEV + 1]
        humidity = first[3 * LEV : 3 * LEV + 1]
        surface = temp_ref[:, lanes]
        scale = 0.6 * jnp.sqrt(wind_east * wind_east + wind_north * wind_north + 1.0)
        flux_ref[0:1, lanes] = scale * (air_temp - surface)
        flux_ref[1:2, lanes] = scale * (humidity - 0.5 * jnp.exp(0.2 * surface))
        flux_ref[2:3, lanes] = scale * (wind_east - current_ref[0:1, lanes])
        flux_ref[3:4, lanes] = scale * (wind_north - current_ref[1:2, lanes])

    copies = []
    phases = 4
    for phase in range(phases):
        some = range(phase * blocks // phases, (phase + 1) * blocks // phases)
        for b in some:
            block(b)
        for b in some:
            lanes = pl.ds(b * LANES, LANES)
            copies.append(pltpu.make_async_copy(out_ref.at[b], out_hbm.at[:, lanes], sems.at[b]))
            copies[-1].start()
    copies.append(pltpu.make_async_copy(flux_ref, flux_hbm, sems.at[blocks]))
    copies[-1].start()
    for copy in copies:
        copy.wait()


def vmem():
    return pl.BlockSpec(memory_space=pltpu.VMEM)


def smem():
    return pl.BlockSpec(memory_space=pltpu.SMEM)


def hbm():
    return pl.BlockSpec(memory_space=pltpu.HBM)


def in_hbm(x):
    return pltpu.with_memory_space_constraint(x, pltpu.HBM)


def params(mib):
    return pltpu.CompilerParams(vmem_limit_bytes=mib * MIB)


def exchange(flat, devices):
    shaped = flat.reshape(devices, flat.shape[0] // devices // 4, 4, LANES)
    moved = lax.all_to_all(shaped, "comp", split_axis=0, concat_axis=0, tiled=True)
    return moved.reshape(flat.shape)


def shards(
    src_fields, weights, block_src, send_src, coupler_send, ocean_from, surface_temp, ocean_current
):
    devices = lax.axis_size("comp")
    slots, slots2 = send_src.shape[1], coupler_send.shape[1]
    blocks, block_rows, block_cols = weights.shape
    rows, columns = src_fields.shape
    cells = ocean_from.shape[0]
    total = devices * slots
    coupled = blocks * block_rows
    narrow, wide = slots * 5 // 2, slots2 * 5 // 2
    dma = pltpu.SemaphoreType.DMA

    outgoing = pl.pallas_call(
        gather_kernel,
        out_shape=jax.ShapeDtypeStruct((devices * narrow, LANES), F32),
        in_specs=[hbm(), hbm()],
        out_specs=hbm(),
        scratch_shapes=[
            pltpu.VMEM((slots, devices), I32),
            pltpu.VMEM((columns, rows), F32),
            pltpu.VMEM((devices * narrow, LANES), F32),
            dma((2,)),
            dma((4,)),
        ],
        compiler_params=params(16),
        name="gather_rows",
    )(in_hbm(send_src.T), in_hbm(src_fields.T))
    received = exchange(outgoing, devices)

    kept = 2 * rows
    spread, take, table = pl.pallas_call(
        lambda *refs: spread_kernel(slots, *refs),
        out_shape=[
            jax.ShapeDtypeStruct((coupled, 2 * kept), BF16),
            jax.ShapeDtypeStruct((2, kept), I32),
            jax.ShapeDtypeStruct((2, coupled), I32),
        ],
        in_specs=[vmem(), vmem(), vmem()],
        out_specs=[vmem(), vmem(), vmem()],
        scratch_shapes=[pltpu.VMEM((blocks, total, block_cols), BF16)],
        compiler_params=params(24),
        name="spread_weights",
    )(block_src, weights, coupler_send.T)

    leaving = pl.pallas_call(
        lambda *refs: couple_kernel(slots, slots2, *refs),
        out_shape=jax.ShapeDtypeStruct((devices * wide, LANES), F32),
        in_specs=[vmem(), vmem(), vmem(), vmem()],
        out_specs=hbm(),
        scratch_shapes=[
            pltpu.SMEM((2, kept), I32),
            pltpu.SMEM((2, coupled), I32),
            pltpu.VMEM((devices * slots, LANES), F32),
            pltpu.VMEM((3 * kept, 3 * LANES), BF16),
            pltpu.VMEM((devices * 2 * slots2, LANES), F32),
            pltpu.VMEM((devices * slots2 // 2, LANES), F32),
            pltpu.VMEM((devices * slots2, LANES), F32),
            pltpu.VMEM((8, coupled // 8, 2 * LANES), F32),
            pltpu.VMEM((8, coupled // 8, LANES), F32),
            dma((2,)),
            dma((4,)),
            dma((4,)),
        ],
        compiler_params=params(24),
        name="couple",
    )(take, table, spread, received)
    arrived = exchange(leaving, devices)

    base = (ocean_from // slots2) * wide
    position = ocean_from % slots2
    half = slots2 // 2
    head = base + position
    tail = base + 2 * slots2 + position % half
    lower = (position < half).astype(I32)[None]
    remapped, fluxes = pl.pallas_call(
        lambda *refs: place_kernel(slots2, *refs),
        out_shape=[jax.ShapeDtypeStruct((columns, cells), F32), jax.ShapeDtypeStruct((4, cells), F32)],
        in_specs=[smem(), vmem(), vmem(), vmem(), vmem()],
        out_specs=[hbm(), hbm()],
        scratch_shapes=[
            pltpu.VMEM((cells // LANES, columns, LANES), F32),
            pltpu.VMEM((4, cells), F32),
            dma((cells // LANES + 1,)),
        ],
        compiler_params=params(16),
        name="place",
    )(jnp.stack([head, tail]), lower, surface_temp[None], ocean_current, arrived)
    return (remapped.T, fluxes)


def solution(mesh):
    return jax.shard_map(
        shards,
        mesh=mesh,
        in_specs=(
            P("comp", None),
            P("comp", None, None),
            P("comp", None),
            P("comp", None),
            P("comp", None),
            P("comp"),
            P("comp"),
            P(None, "comp"),
        ),
        out_specs=(P("comp", None), P(None, "comp")),
        check_vma=False,
    )
```

```python
import jax
import jax.numpy as jnp
from jax import lax
from jax.experimental import pallas as pl
from jax.experimental.pallas import tpu as pltpu
from jax.sharding import PartitionSpec as P

LEV = 8
LANES = 128
HALF = LANES // 2
SUB = 8
BF16 = jnp.bfloat16
F32 = jnp.float32
I32 = jnp.int32
MIB = 1024 * 1024


def split(x):
    high = x.astype(BF16)
    low = (x - high.astype(F32)).astype(BF16)
    return high, low


def dot(a, b, dims):
    return lax.dot_general(a, b, (dims, ((), ())), preferred_element_type=F32)


def iota(shape, dim):
    return lax.broadcasted_iota(I32, shape, dim)


def one_hot(mask):
    return jnp.where(mask, 1.0, 0.0).astype(BF16)


def gather_kernel(send_hbm, src_hbm, out_hbm, send_ref, src_ref, out_ref, in_sems, out_sems):
    slots, devices = send_ref.shape
    columns, rows = src_ref.shape
    pieces = in_sems.shape[0] - 1
    piece = columns // pieces
    send_copy = pltpu.make_async_copy(send_hbm, send_ref, in_sems.at[pieces])
    send_copy.start()
    copies = []
    for i in range(pieces):
        part = pl.ds(i * piece, piece)
        copies.append(pltpu.make_async_copy(src_hbm.at[part], src_ref.at[part], in_sems.at[i]))
        copies[-1].start()
    send_copy.wait()
    picks = send_ref[...].T
    stride = slots * 5 // 2
    groups = out_sems.shape[0]
    each = devices // groups
    hots = []
    for g in range(groups):
        some = picks[g * each : (g + 1) * each]
        hots.append(
            jnp.concatenate(
                [one_hot(iota((each, rows), 1) == some[:, k : k + 1]) for k in range(slots)], axis=0
            )
        )
    for copy in copies:
        copy.wait()
    high, low = split(src_ref[...])
    copies = []
    for g in range(groups):
        taken = dot(hots[g], high, ((1,), (1,))) + dot(hots[g], low, ((1,), (1,)))
        taken = [taken[k * each : (k + 1) * each] for k in range(slots)]
        base = g * each * stride
        for k in range(slots):
            out_ref[pl.ds(base + k, each, stride=stride), :] = taken[k][:, :LANES]
            out_ref[pl.ds(base + slots + k, each, stride=stride), :] = taken[k][:, LANES : 2 * LANES]
        for k in range(slots // 2):
            both = jnp.concatenate(
                [taken[k][:, 2 * LANES :], taken[k + slots // 2][:, 2 * LANES :]], axis=1
            )
            out_ref[pl.ds(base + 2 * slots + k, each, stride=stride), :] = both
        part = pl.ds(base, each * stride)
        copies.append(pltpu.make_async_copy(out_ref.at[part], out_hbm.at[part], out_sems.at[g]))
        copies[-1].start()
    for copy in copies:
        copy.wait()


def spread_kernel(slots, src_ref, weights_ref, send_ref, spread_ref, take_ref, table_ref, hot_ref):
    blocks, block_rows, block_cols = weights_ref.shape
    coupled, kept = spread_ref.shape[0], spread_ref.shape[1] // 2
    total = hot_ref.shape[1]
    senders = total // slots
    counts = jnp.zeros((SUB, total), F32)
    for b in range(blocks):
        hot_ref[b] = one_hot(iota((total, block_cols), 0) == src_ref[b : b + 1, :])
        counts += dot(jnp.ones((SUB, block_cols), BF16), hot_ref[b], ((1,), (1,)))
    used = counts > 0
    earlier = one_hot(iota((total, total), 0) < iota((total, total), 1))
    rank = dot(one_hot(used), earlier, ((1,), (0,))).astype(I32)
    first_row = iota((SUB, total), 0) == 0
    digits = jnp.where(first_row, rank // 16, rank % 16).astype(BF16)
    for b in range(blocks):
        digit = dot(digits, hot_ref[b], ((1,), (0,))).astype(I32)
        column = digit[0:1] * 16 + digit[1:2]
        hot = one_hot(iota((kept, block_cols), 0) == column)
        high, low = split(weights_ref[b])
        summed = dot(high, hot, ((1,), (1,))) + dot(low, hot, ((1,), (1,)))
        high, low = split(summed)
        for i, part in enumerate((high, low)):
            spread_ref[b * block_rows : (b + 1) * block_rows, i * kept : (i + 1) * kept] = part

    slot = iota((SUB, total), 1)
    digits = jnp.where(first_row, slot // slots, slot % slots).astype(BF16)
    listed = jnp.where(used[:1], rank[:1], -1)
    kept_hot = one_hot(iota((kept, total), 0) == listed)
    digit = dot(digits, kept_hot, ((1,), (1,))).astype(I32)
    sender, k = digit[0:1], digit[1:2]
    half = slots // 2
    take_ref[0:1, :] = sender * (slots * 5 // 2) + k
    take_ref[1:2, :] = (k // half) * (half * senders) + (k % half) * senders + sender

    slots2, oceans = send_ref.shape
    send = send_ref[...]
    ocean, position = jnp.zeros((SUB, coupled), F32), jnp.zeros((SUB, coupled), F32)
    for k in range(slots2):
        hot = one_hot(iota((coupled, oceans), 0) == send[k : k + 1])
        ocean += dot(iota((SUB, oceans), 1).astype(BF16), hot, ((1,), (1,)))
        position += dot(jnp.full((SUB, oceans), k, BF16), hot, ((1,), (1,)))
    real = iota((1, coupled), 1) > 0
    ocean = jnp.where(real, ocean[:1].astype(I32), 0)
    position = jnp.where(real, position[:1].astype(I32), 0)
    half = slots2 // 2
    table_ref[0:1, :] = ocean * (2 * slots2) + position
    table_ref[1:2, :] = (position // half) * (oceans * half) + ocean * half + position % half


def couple_kernel(
    slots, slots2, take_any, table_any, spread_ref, recv_ref, out_hbm,
    take_ref, table_ref, double_ref, stacked_ref,
    head_ref, tail_ref, end_ref, block_ref, end_block_ref, table_sems, head_sems, tail_sems,
):
    coupled, kept = spread_ref.shape[0], spread_ref.shape[1] // 2
    take_copy = pltpu.make_async_copy(take_any, take_ref, table_sems.at[0])
    take_copy.start()
    table_copy = pltpu.make_async_copy(table_any, table_ref, table_sems.at[1])
    table_copy.start()
    blocks = block_ref.shape[0]
    each = coupled // blocks
    stride = slots * 5 // 2
    senders = recv_ref.shape[0] // stride
    left = iota((senders, LANES), 1) < HALF
    for k in range(slots // 2):
        both = recv_ref[pl.ds(2 * slots + k, senders, stride=stride), :]
        turned = pltpu.roll(both, HALF, 1)
        double_ref[pl.ds(k * senders, senders), :] = jnp.where(left, both, turned)
        double_ref[pl.ds((slots // 2 + k) * senders, senders), :] = jnp.where(left, turned, both)
    take_copy.wait()

    group = 4
    row = iota((SUB, LANES), 0)

    def pick(ref, slots):
        value = ref[pl.ds(slots[0], SUB, stride=0), :]
        for i in range(1, SUB):
            value = jnp.where(row == i, ref[pl.ds(slots[i], SUB, stride=0), :], value)
        return value

    for base in range(0, kept, 2 * SUB):
        parts = []
        for start in (base, base + SUB):
            heads = [take_ref[0, j] for j in range(start, start + SUB)]
            tails = [take_ref[1, j] for j in range(start, start + SUB)]
            parts.append(
                (pick(recv_ref, heads), pick(recv_ref, [h + slots for h in heads]), pick(double_ref, tails))
            )
        for c in range(3):
            lanes = slice(c * LANES, (c + 1) * LANES)
            high, low = split(jnp.concatenate([parts[0][c], parts[1][c]], axis=0))
            for i, part in enumerate((high, high, low)):
                stacked_ref[i * kept + base : i * kept + base + 2 * SUB, lanes] = part

    contract = ((1,), (0,))

    def product(i, lanes):
        rows = pl.ds(i * each, each)
        return dot(spread_ref[rows], stacked_ref[: 2 * kept, lanes], contract) + dot(
            spread_ref[rows, :kept], stacked_ref[2 * kept :, lanes], contract
        )

    oceans = head_ref.shape[0] // (2 * slots2)

    def scatter(i):
        for base in range(0, each, group):
            rows = range(base, base + group)
            heads = [table_ref[0, i * each + j] for j in rows]
            values = [(block_ref[i, j : j + 1, :LANES], block_ref[i, j : j + 1, LANES:]) for j in rows]
            for head, value in zip(heads, values):
                head_ref[pl.ds(head, 1), :] = value[0]
                head_ref[pl.ds(head + slots2, 1), :] = value[1]

    def scatter_end(i):
        for base in range(0, each, group):
            rows = range(base, base + group)
            tails = [table_ref[1, i * each + j] for j in rows]
            values = [end_block_ref[i, j : j + 1, :] for j in rows]
            for tail, value in zip(tails, values):
                end_ref[pl.ds(tail, 1), :] = value

    head_lanes, tail_lanes = slice(0, 2 * LANES), slice(2 * LANES, 3 * LANES)
    table_copy.wait()
    for i in range(blocks):
        block_ref[i] = product(i, head_lanes)
        if i == 0:
            first = jnp.broadcast_to(block_ref[0, 0:1, :LANES], (slots2, LANES))
            second = jnp.broadcast_to(block_ref[0, 0:1, LANES:], (slots2, LANES))
            for o in range(oceans):
                head_ref[2 * o * slots2 : (2 * o + 1) * slots2, :] = first
                head_ref[(2 * o + 1) * slots2 : (2 * o + 2) * slots2, :] = second
        else:
            scatter(i - 1)
    scatter(blocks - 1)
    pieces = head_sems.shape[0]
    some = oceans // pieces
    copies = []
    head_view = head_ref.reshape(oceans, 2 * slots2, LANES)
    out_view = out_hbm.reshape(oceans, slots2 * 5 // 2, LANES)
    for q in range(pieces):
        part = pl.ds(q * some, some)
        copies.append(
            pltpu.make_async_copy(head_view.at[part], out_view.at[part, : 2 * slots2], head_sems.at[q])
        )
        copies[-1].start()
    for i in range(blocks):
        end_block_ref[i] = product(i, tail_lanes)
        if i == 0:
            end_ref[...] = jnp.broadcast_to(end_block_ref[0, 0:1, :], end_ref.shape)
        else:
            scatter_end(i - 1)
    scatter_end(blocks - 1)
    half = slots2 // 2
    left = iota((some * half, LANES), 1) < HALF
    tail_view = tail_ref.reshape(oceans, half, LANES)
    for q in range(pieces):
        rows = pl.ds(q * some * half, some * half)
        far = pl.ds((oceans + q * some) * half, some * half)
        tail_ref[rows] = jnp.where(left, end_ref[rows], end_ref[far])
        part = pl.ds(q * some, some)
        copies.append(
            pltpu.make_async_copy(tail_view.at[part], out_view.at[part, 2 * slots2 :], tail_sems.at[q])
        )
        copies[-1].start()
    for copy in copies:
        copy.wait()


def place_kernel(
    slots2, slot_ref, lower_ref, temp_ref, current_ref, arrived_ref, out_hbm, flux_hbm,
    out_ref, flux_ref, sems,
):
    blocks = sems.shape[0] - 1
    row = iota((SUB, LANES), 0)

    def pick(slots):
        value = arrived_ref[pl.ds(slots[0], SUB, stride=0), :]
        for i in range(1, SUB):
            value = jnp.where(row == i, arrived_ref[pl.ds(slots[i], SUB, stride=0), :], value)
        return value

    def block(b):
        base = b * LANES
        first, second, third = [], [], []
        for j in range(base, base + LANES, SUB):
            heads = [slot_ref[0, j + i] for i in range(SUB)]
            tails = [slot_ref[1, j + i] for i in range(SUB)]
            first.append(pick(heads))
            second.append(pick([h + slots2 for h in heads]))
            third.append(pick(tails))
        first, second, third = (jnp.concatenate(x, axis=0).T for x in (first, second, third))
        lanes = pl.ds(base, LANES)
        out_ref[b, :LANES, :] = first
        out_ref[b, LANES : 2 * LANES, :] = second
        out_ref[b, 2 * LANES :, :] = jnp.where(lower_ref[:, lanes] > 0, third[:HALF], third[HALF:])
        wind_east = first[0:1]
        wind_north = first[LEV : LEV + 1]
        air_temp = first[2 * LEV : 2 * LEV + 1]
        humidity = first[3 * LEV : 3 * LEV + 1]
        surface = temp_ref[:, lanes]
        scale = 0.6 * jnp.sqrt(wind_east * wind_east + wind_north * wind_north + 1.0)
        flux_ref[0:1, lanes] = scale * (air_temp - surface)
        flux_ref[1:2, lanes] = scale * (humidity - 0.5 * jnp.exp(0.2 * surface))
        flux_ref[2:3, lanes] = scale * (wind_east - current_ref[0:1, lanes])
        flux_ref[3:4, lanes] = scale * (wind_north - current_ref[1:2, lanes])

    copies = []
    phases = 8
    for phase in range(phases):
        some = range(phase * blocks // phases, (phase + 1) * blocks // phases)
        for b in some:
            block(b)
        for b in some:
            lanes = pl.ds(b * LANES, LANES)
            copies.append(pltpu.make_async_copy(out_ref.at[b], out_hbm.at[:, lanes], sems.at[b]))
            copies[-1].start()
    copies.append(pltpu.make_async_copy(flux_ref, flux_hbm, sems.at[blocks]))
    copies[-1].start()
    for copy in copies:
        copy.wait()


def vmem():
    return pl.BlockSpec(memory_space=pltpu.VMEM)


def smem():
    return pl.BlockSpec(memory_space=pltpu.SMEM)


def hbm():
    return pl.BlockSpec(memory_space=pltpu.HBM)


def in_hbm(x):
    return pltpu.with_memory_space_constraint(x, pltpu.HBM)


def params(mib):
    return pltpu.CompilerParams(vmem_limit_bytes=mib * MIB)


def exchange(flat, devices):
    shaped = flat.reshape(devices, flat.shape[0] // devices // 4, 4, LANES)
    moved = lax.all_to_all(shaped, "comp", split_axis=0, concat_axis=0, tiled=True)
    return moved.reshape(flat.shape)


def shards(
    src_fields, weights, block_src, send_src, coupler_send, ocean_from, surface_temp, ocean_current
):
    devices = lax.axis_size("comp")
    slots, slots2 = send_src.shape[1], coupler_send.shape[1]
    blocks, block_rows, block_cols = weights.shape
    rows, columns = src_fields.shape
    cells = ocean_from.shape[0]
    total = devices * slots
    coupled = blocks * block_rows
    narrow, wide = slots * 5 // 2, slots2 * 5 // 2
    dma = pltpu.SemaphoreType.DMA

    outgoing = pl.pallas_call(
        gather_kernel,
        out_shape=jax.ShapeDtypeStruct((devices * narrow, LANES), F32),
        in_specs=[hbm(), hbm()],
        out_specs=hbm(),
        scratch_shapes=[
            pltpu.VMEM((slots, devices), I32),
            pltpu.VMEM((columns, rows), F32),
            pltpu.VMEM((devices * narrow, LANES), F32),
            dma((2,)),
            dma((4,)),
        ],
        compiler_params=params(16),
        name="gather_rows",
    )(in_hbm(send_src.T), in_hbm(src_fields.T))
    received = exchange(outgoing, devices)

    kept = 2 * rows
    spread, take, table = pl.pallas_call(
        lambda *refs: spread_kernel(slots, *refs),
        out_shape=[
            jax.ShapeDtypeStruct((coupled, 2 * kept), BF16),
            jax.ShapeDtypeStruct((2, kept), I32),
            jax.ShapeDtypeStruct((2, coupled), I32),
        ],
        in_specs=[vmem(), vmem(), vmem()],
        out_specs=[vmem(), vmem(), vmem()],
        scratch_shapes=[pltpu.VMEM((blocks, total, block_cols), BF16)],
        compiler_params=params(24),
        name="spread_weights",
    )(block_src, weights, coupler_send.T)

    leaving = pl.pallas_call(
        lambda *refs: couple_kernel(slots, slots2, *refs),
        out_shape=jax.ShapeDtypeStruct((devices * wide, LANES), F32),
        in_specs=[vmem(), vmem(), vmem(), vmem()],
        out_specs=hbm(),
        scratch_shapes=[
            pltpu.SMEM((2, kept), I32),
            pltpu.SMEM((2, coupled), I32),
            pltpu.VMEM((devices * slots, LANES), F32),
            pltpu.VMEM((3 * kept, 3 * LANES), BF16),
            pltpu.VMEM((devices * 2 * slots2, LANES), F32),
            pltpu.VMEM((devices * slots2 // 2, LANES), F32),
            pltpu.VMEM((devices * slots2, LANES), F32),
            pltpu.VMEM((8, coupled // 8, 2 * LANES), F32),
            pltpu.VMEM((8, coupled // 8, LANES), F32),
            dma((2,)),
            dma((4,)),
            dma((4,)),
        ],
        compiler_params=params(24),
        name="couple",
    )(take, table, spread, received)
    arrived = exchange(leaving, devices)

    base = (ocean_from // slots2) * wide
    position = ocean_from % slots2
    half = slots2 // 2
    head = base + position
    tail = base + 2 * slots2 + position % half
    lower = (position < half).astype(I32)[None]
    remapped, fluxes = pl.pallas_call(
        lambda *refs: place_kernel(slots2, *refs),
        out_shape=[jax.ShapeDtypeStruct((columns, cells), F32), jax.ShapeDtypeStruct((4, cells), F32)],
        in_specs=[smem(), vmem(), vmem(), vmem(), vmem()],
        out_specs=[hbm(), hbm()],
        scratch_shapes=[
            pltpu.VMEM((cells // LANES, columns, LANES), F32),
            pltpu.VMEM((4, cells), F32),
            dma((cells // LANES + 1,)),
        ],
        compiler_params=params(16),
        name="place",
    )(jnp.stack([head, tail]), lower, surface_temp[None], ocean_current, arrived)
    return (remapped.T, fluxes)


def solution(mesh):
    return jax.shard_map(
        shards,
        mesh=mesh,
        in_specs=(
            P("comp", None),
            P("comp", None, None),
            P("comp", None),
            P("comp", None),
            P("comp", None),
            P("comp"),
            P("comp"),
            P(None, "comp"),
        ),
        out_specs=(P("comp", None), P(None, "comp")),
        check_vma=False,
    )
```
